32 devices in a mesh: depth: 16 (over z, x, core), band: 2 (over y).
Axes of the slice: x: 2, y: 2, z: 4, core: 2. Of those that a mesh axis runs over, the one named last changes fastest.
Arguments:
- volume: int32 [64, 64, 1024], P('depth', 'band'), may hold values from 0 to 255
- tf_table: int32 [4, 256], replicated, may hold values from 0 to 255
- view_code: int32 [2, 4], replicated, may hold values from -20 to 20
Outputs:
- final_image: float32 [2, 1024, 4, 64], P(None, 'depth', None, 'band')
The draws below stay inside these ranges and needn't reach their ends.
All inputs are finite; a program needn't handle non-finite values.
Results may differ from the reference program's by a relative error of at most 0.0014.
Values may be sent and summed in bfloat16 or wider, within the bound.
A program may use at most 64 MiB of HBM per device.

```python
import jax
import jax.numpy as jnp
from jax import lax

NX = 1024
VIEWS = 2
LEVELS = 256
QMAX = 20
MARGIN = 16
NY = 64
NZ = 64


def place_ends(values, stream_key, low, high):
    index_at = [jax.random.randint(jax.random.fold_in(stream_key, axis), (), 0, length) for axis, length in enumerate(values.shape)]
    widest = values.shape.index(max(values.shape))
    next_to = index_at[:widest] + [(index_at[widest] + 1) % values.shape[widest]] + index_at[widest + 1:]
    return values.at[tuple(index_at)].set(low).at[tuple(next_to)].set(high)


def setup_inputs(seed: int = 0) -> dict:
    seeds = jax.random.split(jax.random.key(seed), 4)
    return {
        "volume": place_ends(jax.random.randint(seeds[0], (NZ, NY, NX), 0, LEVELS), jax.random.fold_in(seeds[0], 1), 0, LEVELS - 1).astype(jnp.int32),
        "tf_table": place_ends(jax.random.randint(seeds[1], (4, LEVELS), 0, 256), jax.random.fold_in(seeds[1], 1), 0, 255).astype(jnp.int32),
        "view_code": place_ends(jax.random.randint(seeds[2], (VIEWS, 4), -QMAX, QMAX + 1), jax.random.fold_in(seeds[2], 1), -QMAX, QMAX).astype(jnp.int32),
    }


tap_steps = (-2, -1, 0, 1, 2, 3)


def lanczos(offset):
    return jnp.where(jnp.abs(offset) < 3.0, jnp.sinc(offset) * jnp.sinc(offset / 3.0), 0.0)


def split_offset(coefficient, position, length, lift=0):
    numerator = coefficient * (2 * position + 1 - length) + lift * length
    integer_part = (numerator // (2 * length)).astype(jnp.int32)
    fraction = (numerator - integer_part * (2 * length)).astype(jnp.float32) / (2.0 * length)
    return integer_part, fraction


def make_palette(tf_table, depth_count):
    table_float = tf_table.astype(jnp.float32)
    opacity = table_float[3] / (64.0 * depth_count)
    premult = table_float[0:3] / 255.0 * opacity
    return jnp.concatenate([premult, opacity[None]], axis=0).astype(jnp.bfloat16)


def shear_taps(source, integer_part, fraction, along, margin):
    extent = source.shape[along]
    widths = [(0, 0)] * source.ndim
    widths[along] = (margin, margin)
    padded = jnp.pad(source.astype(jnp.float32), widths)
    accumulated = jnp.zeros(source.shape, jnp.float32)
    for step_value in tap_steps:
        tap_weight = lax.optimization_barrier(lanczos(fraction - step_value).astype(jnp.bfloat16))
        start = (margin + integer_part + step_value).astype(jnp.int32)
        shifted = lax.dynamic_slice_in_dim(padded, start, extent, along)
        accumulated = accumulated + tap_weight.astype(jnp.float32) * shifted
    return accumulated


def render(volume, palette, params):
    facing = params[3] >= 0

    def advance(picture, slice_step):
        depth_index = jnp.where(facing, slice_step, NZ - 1 - slice_step).astype(jnp.int32)
        voxels = lax.dynamic_index_in_dim(volume, depth_index, 0, keepdims=False)
        classified = jnp.take(palette, voxels, axis=1)
        whole_x, frac_x = split_offset(params[0], depth_index, NZ)
        whole_y, frac_y = split_offset(params[1], depth_index, NZ)
        row_sheared = shear_taps(classified, whole_x, frac_x, 2, MARGIN).astype(jnp.bfloat16)
        row_sheared = lax.optimization_barrier(row_sheared)
        sheared = shear_taps(row_sheared, whole_y, frac_y, 1, MARGIN)
        return picture + (1.0 - picture[3:4]) * sheared, None

    start_picture = jnp.zeros((4, NY, NX), jnp.float32)
    picture, unused = lax.scan(advance, start_picture, jnp.arange(NZ, dtype=jnp.int32))
    return picture


def warp_columns(picture, coefficient):
    columns = jnp.arange(NX, dtype=jnp.int32)
    integer_part, fraction = split_offset(coefficient, columns, NX, 1)
    accumulated = jnp.zeros(picture.shape, jnp.float32)
    for step_value in tap_steps:
        tap_weight = lanczos(fraction - step_value)
        source_index = (columns + integer_part + step_value).astype(jnp.int32)
        inside = (source_index >= 0) & (source_index < NX)
        picked = jnp.take(picture, jnp.clip(source_index, 0, NX - 1), axis=2)
        accumulated = accumulated + jnp.where(inside, tap_weight, 0.0) * picked
    return jnp.transpose(accumulated, (2, 0, 1))


def reference(volume, tf_table, view_code):
    palette = make_palette(tf_table, NZ)
    finals = []
    for view_index in range(VIEWS):
        params = view_code[view_index]
        picture = render(volume, palette, params)
        finals.append(warp_columns(picture, params[2]))
    return jnp.stack(finals)
```

```python
import functools

import jax
import jax.numpy as jnp
from jax import lax
from jax.experimental import pallas as pl
from jax.experimental.pallas import tpu as pltpu

VIEWS = 2
MARGIN = 16
PAD = 128
LANES = 128
LAG1 = 2
LAG2 = 6
MESH = pl.DeviceIdType.MESH


def lanczos(t):
    def sinc(u):
        x = jnp.float32(jnp.pi) * u
        safe = jnp.where(u == 0.0, 1.0, x)
        return jnp.where(u == 0.0, 1.0, jnp.sin(safe) / safe)

    return jnp.where(jnp.abs(t) < 3.0, sinc(t) * sinc(t / 3.0), 0.0)


def take(table_row, index):
    table = jnp.broadcast_to(table_row, index.shape)
    return jnp.take_along_axis(table, index, axis=1, mode="promise_in_bounds")


def replicate_alpha(part, lane):
    width = LANES // 4
    alpha = jnp.where(lane >= 3 * width, part, 0.0)
    alpha = alpha + pltpu.roll(alpha, 2 * width, 1)
    return alpha + pltpu.roll(alpha, width, 1)


def kernel(
    sizes, code_hbm, volume_hbm, tf_hbm, out_ref,
    code_ref, volume_ref, tf_ref, edge_ref, halo_ref, own_ref, far_ref, wx_ref, wy_ref, moved_ref, sheared_ref, picture_ref,
    s1_ref, r1_ref, s2_ref, r2_ref, k2_ref, s3_ref, r3_ref, mine_ref,
    load_sem, halo_send, halo_recv, send1, recv1, send2, recv2, send3, recv3,
):
    depth_size, band_size = sizes
    slabs, rows, extent = volume_ref.shape
    stations = depth_size // 4
    chunk = extent // stations
    strip = chunk // 4
    reach = chunk + 2 * MARGIN
    piece = strip + MARGIN
    total_depth = slabs * depth_size
    slots = 1 if band_size == 2 else 2
    side = 4 * MARGIN * slots
    d = lax.axis_index("depth")
    band = lax.axis_index("band")
    core = lax.rem(d, 2)
    col = lax.rem(lax.div(d, 2), 2)
    z = lax.div(d, 4)
    peer1 = d + 1 - 2 * core
    peer2 = d + 2 - 4 * col
    half = stations // 2
    low = 1 - lax.div(z, half)

    def mirrored(i):
        return i * low + (stations - 1 - i) * (1 - low)

    def station(step):
        if step < half:
            return mirrored(stations - 1 - step)
        if step == stations - 1:
            return z
        u, inner = step - half, half - 1 - mirrored(z)
        return mirrored(jnp.where(u < inner, half - 1 - u, u - inner))

    def at_depth(i):
        return (i, band)

    barrier = pltpu.get_barrier_semaphore()

    def greet(device):
        pl.semaphore_signal(barrier, inc=1, device_id=device, device_id_type=MESH)

    @pl.when(band > 0)
    def _():
        greet((d, band - 1))

    @pl.when(band < band_size - 1)
    def _():
        greet((d, band + 1))

    greet(at_depth(peer1))
    greet(at_depth(peer2))
    for k in range(1, stations):
        greet(at_depth(lax.rem(z + k, stations) * 4 + lax.rem(d, 4)))

    loads = [
        pltpu.make_async_copy(source, target, load_sem.at[i])
        for i, (source, target) in enumerate(((code_hbm, code_ref), (volume_hbm, volume_ref), (tf_hbm, tf_ref)))]
    for load in loads:
        load.start()

    for s in range(slabs):
        for ref in (own_ref, far_ref):
            zeros = jnp.zeros((ref.shape[1], PAD), jnp.bfloat16)
            ref[s, :, 0:PAD] = zeros
            ref[s, :, PAD + extent : 2 * PAD + extent] = zeros
    r3_ref[z] = jnp.zeros((VIEWS, piece, LANES), jnp.bfloat16)

    loads[0].wait()
    count = VIEWS * slabs
    row_id = lax.broadcasted_iota(jnp.int32, (2 * count, LANES), 0)
    whole = jnp.zeros((2 * count, LANES), jnp.float32)
    frac = jnp.zeros((2 * count, LANES), jnp.float32)
    period = 2 * total_depth
    for axis in range(2):
        for v in range(VIEWS):
            for s in range(slabs):
                position = d * slabs + s
                num = code_ref[v, axis] * (2 * position + 1 - total_depth)
                w = lax.div(num + 64 * period, period) - 64
                f = (num - w * period).astype(jnp.float32) / float(period)
                here = row_id == axis * count + v * slabs + s
                whole = jnp.where(here, w.astype(jnp.float32), whole)
                frac = jnp.where(here, f, frac)
    lane_f = lax.broadcasted_iota(jnp.int32, (2 * count, LANES), 1).astype(jnp.float32)
    taps = lanczos(frac - (lane_f - float(LANES // 2) - whole))

    lane16 = lax.broadcasted_iota(jnp.int32, (16, LANES), 1)
    row16 = lax.broadcasted_iota(jnp.int32, (16, LANES), 0)
    diagonal = (lane16 - row16) & (LANES - 1)
    zero_tile = jnp.zeros((16, LANES), jnp.bfloat16)

    def column_weights():
        for v in range(VIEWS):
            for s in range(slabs):
                base = take(taps[v * slabs + s : v * slabs + s + 1], diagonal)
                for turn in range(0, LANES, 16):
                    moved = pltpu.roll(base, turn, 1) if turn else base
                    row = v * LANES + turn
                    wx_ref[s, row : row + 16, 0:LANES] = jnp.where(lane16 >= turn, moved, 0.0).astype(jnp.bfloat16)
                    wx_ref[s, row : row + 16, LANES : 2 * LANES] = jnp.where(lane16 < turn, moved, 0.0).astype(jnp.bfloat16)

    def row_weights():
        group = lane16 // rows
        y = lane16 - group * rows
        for v in range(VIEWS):
            for s in range(slabs):
                at = count + v * slabs + s
                parts = [(r, [c * rows + r for c in range(4)]) for r in range(0, rows, 16)]
                if slots == 1:
                    parts.append((jnp.where(band == 0, rows, -MARGIN), [LANES + c * MARGIN for c in range(4)]))
                else:
                    for slot, position in ((0, -MARGIN), (1, rows)):
                        parts.append((position, [LANES + slot * 4 * MARGIN + c * MARGIN for c in range(4)]))
                for position, places in parts:
                    tile = take(taps[at : at + 1], row16 + position - y + LANES // 2)
                    for c in range(4):
                        left = jnp.where(group == c, tile, 0.0).astype(jnp.bfloat16)
                        right = tile.astype(jnp.bfloat16) if c == 3 else zero_tile
                        for k in range(places[c], LANES if places[c] < LANES else 2 * LANES, side):
                            wy_ref[v * slabs + s, k : k + 16, 0:LANES] = left
                            wy_ref[v * slabs + s, k : k + 16, LANES : 2 * LANES] = right
                            if places[c] < LANES:
                                break

    column_weights()

    loads[1].wait()
    for s in range(slabs):
        edge_ref[0, s] = volume_ref[s, rows - MARGIN : rows, :].astype(jnp.float32).astype(jnp.bfloat16)
        edge_ref[1, s] = volume_ref[s, 0:MARGIN, :].astype(jnp.float32).astype(jnp.bfloat16)

    def neighbours(i, n):
        return lax.div(i + n - 1, n) + 1 - lax.div(i + 1, n)

    pl.semaphore_wait(
        barrier, 1 + stations + neighbours(band, band_size))

    units, near_units = extent // LANES, chunk // LANES + 1
    cuts = ((units - near_units, units), (units // 2 - 1, units - near_units), (0, units // 2 - 1))

    def lanes_of(g):
        first, last = cuts[g]
        start = first * low + (units - last) * (1 - low)
        return pl.multiple_of(start * LANES, LANES), last - first

    def group_of(ref, slot, g):
        start, width = lanes_of(g)
        return ref.at[slot, :, :, pl.ds(start, width * LANES)]

    def to_next(g):
        return pltpu.make_async_remote_copy(
            group_of(edge_ref, 0, g), group_of(halo_ref, 0, g), halo_send.at[0, g], halo_recv.at[0, g],
            device_id=(d, lax.rem(band + 1, band_size)), device_id_type=MESH)

    def to_previous(g):
        last = slots - 1
        return pltpu.make_async_remote_copy(
            group_of(edge_ref, 1, g), group_of(halo_ref, last, g), halo_send.at[1, g], halo_recv.at[last, g],
            device_id=(d, lax.rem(band + band_size - 1, band_size)), device_id_type=MESH)

    @pl.when(band < band_size - 1)
    def _():
        for g in range(3):
            to_next(g).start()

    @pl.when(band > 0)
    def _():
        for g in range(3):
            to_previous(g).start()

    loads[2].wait()
    table = tf_ref[...]
    words = table[0:1] | (table[1:2] << 8) | (table[2:3] << 16) | (table[3:4] << 24)
    alpha_unit = 1.0 / (64.0 * total_depth)

    def classify(codes):
        low_bits = codes & (LANES - 1)
        first = take(words[:, 0:LANES], low_bits)
        second = take(words[:, LANES : 2 * LANES], low_bits)
        word = jnp.where(codes >= LANES, second, first)
        alpha = lax.shift_right_logical(word, 24).astype(jnp.float32)
        scaled = alpha * (alpha_unit / 255.0)
        colors = [((word >> shift if shift else word) & 255).astype(jnp.float32) * scaled for shift in (0, 8, 16)]
        return [part.astype(jnp.bfloat16) for part in colors + [alpha * alpha_unit]]

    def own_rows(s, carry):
        for r in range(0, rows, 16):
            for x in range(0, extent, LANES):
                for c, part in enumerate(classify(volume_ref[s, r : r + 16, x : x + LANES])):
                    own_ref[s, c * rows + r : c * rows + r + 16, PAD + x : PAD + x + LANES] = part
        return carry

    lax.fori_loop(0, slabs, own_rows, 0)
    row_weights()

    tiles = extent // LANES + 1
    for s in range(slabs):
        for t in range(0, tiles, 2):
            pair = range(t, min(t + 2, tiles))
            data = [own_ref[s, :, u * LANES : (u + 2) * LANES] for u in pair]
            moved = lax.dot_general(
                wx_ref[s], jnp.concatenate(data, axis=0) if len(data) > 1 else data[0],
                (((1,), (1,)), ((), ())), preferred_element_type=jnp.float32).astype(jnp.bfloat16)
            for v in range(VIEWS):
                for i, u in enumerate(pair):
                    moved_ref[v, s, u * LANES : (u + 1) * LANES, 0:LANES] = (
                        moved[v * LANES : (v + 1) * LANES, i * LANES : (i + 1) * LANES])

    has = [band > 0, band < band_size - 1] if slots == 2 else [None]

    def clear(slot):
        row = slot * 4 * MARGIN
        for s in range(slabs):
            far_ref[s, row : row + 4 * MARGIN, PAD : PAD + extent] = jnp.zeros((4 * MARGIN, extent), jnp.bfloat16)

    if slots == 2:
        for slot in range(slots):
            pl.when(jnp.logical_not(has[slot]))(functools.partial(clear, slot))

    def far_rows(g):
        if slots == 1:
            @pl.when(band == 0)
            def _():
                to_next(g).wait()

            @pl.when(band > 0)
            def _():
                to_previous(g).wait()
        else:
            @pl.when(band < band_size - 1)
            def _():
                to_next(g).wait_send()
                to_previous(g).wait_recv()

            @pl.when(band > 0)
            def _():
                to_previous(g).wait_send()
                to_next(g).wait_recv()

        start, width = lanes_of(g)

        def look(slot):
            for s in range(slabs):
                for i in range(width):
                    x = pl.multiple_of(start + i * LANES, LANES)
                    codes = halo_ref[slot, s, :, pl.ds(x, LANES)].astype(jnp.float32).astype(jnp.int32)
                    for c, part in enumerate(classify(codes)):
                        row = slot * 4 * MARGIN + c * MARGIN
                        far_ref[s, row : row + MARGIN, pl.ds(PAD + x, LANES)] = part

        for slot in range(slots):
            if slots == 1:
                look(slot)
            else:
                pl.when(has[slot])(functools.partial(look, slot))

    facing = [code_ref[v, 3] >= 0 for v in range(VIEWS)]
    lane_s = lax.broadcasted_iota(jnp.int32, (piece, LANES), 1)

    def over(ahead, near, far):
        front = jnp.where(ahead, near, far)
        back = jnp.where(ahead, far, near)
        return front + (1.0 - replicate_alpha(front, lane_s)) * back

    def first_copy(step, v):
        return pltpu.make_async_remote_copy(
            s1_ref.at[step, v], r1_ref.at[step, v], send1.at[step, v], recv1.at[step, v],
            device_id=at_depth(peer1), device_id_type=MESH)

    def second_copy(step, v):
        return pltpu.make_async_remote_copy(
            s2_ref.at[step, v], r2_ref.at[step, v], send2.at[step, v], recv2.at[step, v],
            device_id=at_depth(peer2), device_id_type=MESH)

    def third_copy(step, v):
        return pltpu.make_async_remote_copy(
            s3_ref.at[step, v], r3_ref.at[z, v], send3.at[step, v], recv3.at[z, v],
            device_id=at_depth(station(step) * 4 + lax.rem(d, 4)), device_id_type=MESH)

    def offset(v, j):
        first = code_ref[v, 2] * (2 * strip * j + 1 - extent) + extent
        shift = lax.div(first + 128 * extent, 2 * extent) - 64
        return jnp.clip(lax.div(shift + 62, 8) * 8 - 64, -MARGIN, 0) + MARGIN

    def strip_of(step, v, q):
        at = offset(v, station(step) * 4 + q)
        wide = picture_ref[step, v, pl.ds(pl.multiple_of(q * strip, 16), piece + MARGIN), :]
        part = jnp.where(at == 0, wide[0:piece], wide[8 : 8 + piece])
        return jnp.where(at == MARGIN, wide[MARGIN : MARGIN + piece], part)

    near_tiles = chunk // LANES + 1
    lane_t = lax.broadcasted_iota(jnp.int32, (LANES, LANES), 1)

    def far_shear(step):
        start = pl.multiple_of(station(step) * chunk, LANES)
        for s in range(slabs):
            data = [far_ref[s, :, pl.ds(start + t * LANES, 2 * LANES)] for t in range(near_tiles)]
            spare = (-near_tiles * side) % LANES
            if spare:
                data.append(jnp.zeros((spare, 2 * LANES), jnp.bfloat16))
            moved = lax.dot_general(
                wx_ref[s], jnp.concatenate(data, axis=0), (((1,), (1,)), ((), ())), preferred_element_type=jnp.float32)
            for v in range(VIEWS):
                for t in range(near_tiles):
                    at = t * side // LANES * LANES
                    part = moved[v * LANES : (v + 1) * LANES, at : at + LANES]
                    if side < LANES:
                        part = jnp.where(lane_t // side == t * side % LANES // side, part, 0.0)
                    moved_ref[v, s, pl.ds(start + t * LANES, LANES), LANES : 2 * LANES] = part.astype(jnp.bfloat16)

    def render(step, v):
        start = pl.multiple_of(station(step) * chunk + LANES // 2 - MARGIN, 16)
        for s in range(slabs):
            sheared_ref[v, s] = jnp.dot(
                moved_ref[v, s, pl.ds(start, reach), :], wy_ref[v * slabs + s], preferred_element_type=jnp.float32)
        for q in range(0, reach, 32):
            part = slice(q, q + 32)
            picture = None
            for k in range(slabs):
                at = jnp.where(facing[v], slabs - 1 - k, k)
                color = sheared_ref[v, at, part, 0:LANES]
                if picture is None:
                    picture = color
                else:
                    picture = color + (1.0 - sheared_ref[v, at, part, LANES : 2 * LANES]) * picture
            picture_ref[step, v, part] = picture
        for h in range(2):
            s1_ref[step, v, h] = strip_of(step, v, 2 * h + 1 - core).astype(jnp.bfloat16)
        first_copy(step, v).start()

    def merge1(step, v):
        first_copy(step, v).wait()
        ahead = (core == 0) == facing[v]
        for h, keep in ((1 - col, False), (col, True)):
            near = strip_of(step, v, 2 * h + core)
            both = over(ahead, near, r1_ref[step, v, h].astype(jnp.float32))
            if keep:
                k2_ref[step, v] = both
            else:
                s2_ref[step, v] = both.astype(jnp.bfloat16)
                second_copy(step, v).start()

    def merge2(step, v):
        second_copy(step, v).wait()
        ahead = (col == 0) == facing[v]
        both = over(ahead, k2_ref[step, v], r2_ref[step, v].astype(jnp.float32))
        if step == stations - 1:
            mine_ref[v] = both
        else:
            s3_ref[step, v] = both.astype(jnp.bfloat16)
            third_copy(step, v).start()

    def warp_weights(v):
        column = lax.broadcasted_iota(jnp.int32, (strip, piece), 0)
        source = lax.broadcasted_iota(jnp.int32, (strip, piece), 1) + (offset(v, d) - MARGIN)
        double = float(2 * extent)
        column_in = d * strip + source
        inside = jnp.logical_and(column_in >= 0, column_in < extent)
        num = (code_ref[v, 2] * (2 * (d * strip + column) + 1 - extent) + extent).astype(jnp.float32)
        whole_w = jnp.floor(num / double)
        frac_w = (num - whole_w * double) / double
        tap = lanczos(frac_w - ((source - column).astype(jnp.float32) - whole_w))
        return jnp.where(inside, tap, 0.0)

    parts = [(step, v) for step in range(stations) for v in range(VIEWS)]
    total = len(parts)
    weights = []
    for i in range(total + LAG2):
        if i < total:
            step, v = parts[i]
            if v == 0:
                if step in (0, 1, half):
                    far_rows((0, 1, half).index(step))
                far_shear(step)
            render(step, v)
        if i == total:
            weights = [warp_weights(v) for v in range(VIEWS)]
        if 0 <= i - LAG1 < total:
            merge1(*parts[i - LAG1])
        if 0 <= i - LAG2 < total:
            merge2(*parts[i - LAG2])

    def split(value):
        high = value.astype(jnp.bfloat16)
        return high, (value - high.astype(jnp.float32)).astype(jnp.bfloat16)

    for step in range(stations - 1):
        for v in range(VIEWS):
            third_copy(step, v).wait_send()
    for v in range(VIEWS):
        for k in range(1, stations):
            other = lax.rem(z + k, stations)
            pltpu.make_async_remote_copy(
                s3_ref.at[0, v], r3_ref.at[other, v], send3.at[0, v], recv3.at[other, v],
                device_id=at_depth(other * 4 + lax.rem(d, 4)), device_id_type=MESH).wait_recv()
        layers = [
            jnp.where(z == k, mine_ref[v], r3_ref[k, v].astype(jnp.float32)) for k in range(stations)]
        picture = None
        for k in range(stations):
            part = jnp.where(facing[v], layers[stations - 1 - k], layers[k])
            if picture is None:
                picture = part
            else:
                picture = part + (1.0 - replicate_alpha(part, lane_s)) * picture
        (wh, wl), (ph, plow) = split(weights[v]), split(picture)
        final = (
            jnp.dot(wh, ph, preferred_element_type=jnp.float32)
            + jnp.dot(wh, plow, preferred_element_type=jnp.float32)
            + jnp.dot(wl, ph, preferred_element_type=jnp.float32))
        out_ref[v] = final.T


def body(volume, tf_table, view_code):
    depth_size, band_size = lax.axis_size("depth"), lax.axis_size("band")
    slabs, rows, extent = volume.shape
    stations = depth_size // 4
    chunk = extent // stations
    strip = chunk // 4
    reach = chunk + 2 * MARGIN
    piece = strip + MARGIN
    slots = 1 if band_size == 2 else 2
    padded = extent + 2 * PAD
    bf16, f32 = jnp.bfloat16, jnp.float32
    vmem, anywhere = pl.BlockSpec(memory_space=pltpu.VMEM), pl.BlockSpec(memory_space=pl.ANY)
    dma = pltpu.SemaphoreType.DMA
    out = pl.pallas_call(
        functools.partial(kernel, (depth_size, band_size)),
        out_shape=jax.ShapeDtypeStruct((VIEWS, LANES, strip), f32),
        in_specs=[anywhere] * 3,
        out_specs=vmem,
        scratch_shapes=[
            pltpu.SMEM(view_code.shape, jnp.int32),
            pltpu.VMEM(volume.shape, jnp.int32),
            pltpu.VMEM(tf_table.shape, jnp.int32),
            pltpu.VMEM((2, slabs, MARGIN, extent), bf16),
            pltpu.VMEM((slots, slabs, MARGIN, extent), bf16),
            pltpu.VMEM((slabs, 4 * rows, padded), bf16),
            pltpu.VMEM((slabs, 4 * MARGIN * slots, padded), bf16),
            pltpu.VMEM((slabs, VIEWS * LANES, 2 * LANES), bf16),
            pltpu.VMEM((VIEWS * slabs, 2 * LANES, 2 * LANES), bf16),
            pltpu.VMEM((VIEWS, slabs, extent + LANES, 2 * LANES), bf16),
            pltpu.VMEM((VIEWS, slabs, reach, 2 * LANES), f32),
            pltpu.VMEM((stations, VIEWS, reach, LANES), f32),
            pltpu.VMEM((stations, VIEWS, 2, piece, LANES), bf16),
            pltpu.VMEM((stations, VIEWS, 2, piece, LANES), bf16),
            pltpu.VMEM((stations, VIEWS, piece, LANES), bf16),
            pltpu.VMEM((stations, VIEWS, piece, LANES), bf16),
            pltpu.VMEM((stations, VIEWS, piece, LANES), f32),
            pltpu.VMEM((stations, VIEWS, piece, LANES), bf16),
            pltpu.VMEM((stations, VIEWS, piece, LANES), bf16),
            pltpu.VMEM((VIEWS, piece, LANES), f32),
            dma((3,)), dma((2, 3)), dma((slots, 3)),
        ] + [dma((stations, VIEWS))] * 6,
        compiler_params=pltpu.CompilerParams(collective_id=0, has_side_effects=True),
    )(view_code, volume, tf_table)
    return out.reshape(VIEWS, 4, rows, strip).transpose(0, 3, 1, 2)


def solution(mesh):
    P = jax.sharding.PartitionSpec
    placed = (P("depth", "band", None), P(), P())
    return jax.shard_map(
        body, mesh=mesh, in_specs=placed, out_specs=P(None, "depth", None, "band"), check_vma=False
    )
```

```python
import functools

import jax
import jax.numpy as jnp
from jax import lax
from jax.experimental import pallas as pl
from jax.experimental.pallas import tpu as pltpu

VIEWS = 2
MARGIN = 16
PAD = 128
LANES = 128
MESH = pl.DeviceIdType.MESH


def sin_pi(t):
    nearest = jnp.floor(t + 0.5)
    x = jnp.float32(jnp.pi) * (t - nearest)
    odd = nearest - 2.0 * jnp.floor(0.5 * nearest)
    square = x * x
    series = jnp.float32(-1.0 / 39916800.0)
    for factor in (1.0 / 362880.0, -1.0 / 5040.0, 1.0 / 120.0, -1.0 / 6.0, 1.0):
        series = series * square + jnp.float32(factor)
    return x * series * (1.0 - 2.0 * odd)


def lanczos(t):
    safe = jnp.where(t == 0.0, 1.0, t)
    value = sin_pi(t) * sin_pi(t * jnp.float32(1.0 / 3.0)) * jnp.float32(3.0 / jnp.pi**2) / (safe * safe)
    return jnp.where(jnp.abs(t) < 3.0, jnp.where(t == 0.0, 1.0, value), 0.0)


def take(table_row, index):
    table = jnp.broadcast_to(table_row, index.shape)
    return jnp.take_along_axis(table, index, axis=1, mode="promise_in_bounds")


def replicate_alpha(part, lane):
    alpha = jnp.where(lane % (4 * MARGIN) >= 3 * MARGIN, part, 0.0)
    alpha = alpha + pltpu.roll(alpha, LANES - MARGIN, 1)
    return alpha + pltpu.roll(alpha, LANES - 2 * MARGIN, 1)


def schedule(count, early):
    last = count - 1
    order = []
    for i in range(last):
        order += [("far", i, 0)] * early + [("render", i, 0)]
    order += [("merge1", 0, 0)]
    for i in range(last):
        order += [("far", i, 1)] * (1 - early)
        if i == 0:
            order += [("merge1", k, 0) for k in range(1, last)]
        order += [("render", i, 1)]
        if i > 0:
            order += [("merge1", i - 1, 1)]
    order += [("merge2", 0, 0)]
    order += [("far", last, 0)] + [("render", last, 0), ("merge1", last - 1, 1), ("render", last, 1)]
    order += [("merge2", k, 0) for k in range(1, last)] + [("merge1", last, 0)]
    order += [("merge2", k, 1) for k in range(last - 1)] + [("merge1", last, 1), ("merge2", last - 1, 1)]
    order += [("warp", 0, 0), ("merge2", last, 0), ("finish", 0, 0), ("merge2", last, 1)]
    return order + [("finish", 0, 1)]


def kernel(
    sizes, code_hbm, volume_hbm, tf_hbm, out_ref,
    code_ref, volume_ref, tf_ref, edge_ref, halo_ref, own_ref, far_ref, wx_ref, wy_ref, moved_ref, sheared_ref, picture_ref,
    s1_ref, r1_ref, s2_ref, r2_ref, k2_ref, s3_ref, r3_ref, mine_ref,
    load_sem, halo_send, halo_recv, send1, recv1, send2, recv2, send3, recv3,
):
    depth_size, band_size = sizes
    slabs, rows, extent = volume_ref.shape
    stations = depth_size // 4
    chunk = extent // stations
    strip = chunk // 4
    reach = chunk + 2 * MARGIN
    piece = strip + MARGIN
    total_depth = slabs * depth_size
    slots = 1 if band_size == 2 else 2
    side = 4 * MARGIN * slots
    d = lax.axis_index("depth")
    band = lax.axis_index("band")
    core = lax.rem(d, 2)
    col = lax.rem(lax.div(d, 2), 2)
    z = lax.div(d, 4)
    peer1 = d + 1 - 2 * core
    peer2 = d + 2 - 4 * col
    half = stations // 2
    low = 1 - lax.div(z, half)

    def mirrored(i):
        return i * low + (stations - 1 - i) * (1 - low)

    def station(step):
        if step < half:
            return mirrored(stations - 1 - step)
        if step == stations - 1:
            return z
        u, inner = step - half, half - 1 - mirrored(z)
        return mirrored(jnp.where(u < inner, half - 1 - u, u - inner))

    def at_depth(i):
        return (i, band)

    barrier = pltpu.get_barrier_semaphore()

    def greet(device):
        pl.semaphore_signal(barrier, inc=1, device_id=device, device_id_type=MESH)

    @pl.when(band > 0)
    def _():
        greet((d, band - 1))

    @pl.when(band < band_size - 1)
    def _():
        greet((d, band + 1))

    greet(at_depth(peer1))
    greet(at_depth(peer2))
    for k in range(1, stations):
        greet(at_depth(lax.rem(z + k, stations) * 4 + lax.rem(d, 4)))

    loads = [
        pltpu.make_async_copy(source, target, load_sem.at[i])
        for i, (source, target) in enumerate(((code_hbm, code_ref), (volume_hbm, volume_ref), (tf_hbm, tf_ref)))]
    for load in loads:
        load.start()

    for s in range(slabs):
        for ref in (own_ref, far_ref):
            zeros = jnp.zeros((ref.shape[1], PAD), jnp.bfloat16)
            ref[s, :, 0:PAD] = zeros
            ref[s, :, PAD + extent : 2 * PAD + extent] = zeros
    r3_ref[z] = jnp.zeros((VIEWS, piece, LANES), jnp.bfloat16)

    loads[0].wait()
    count = VIEWS * slabs
    row_id = lax.broadcasted_iota(jnp.int32, (2 * count, LANES), 0)
    whole = jnp.zeros((2 * count, LANES), jnp.float32)
    frac = jnp.zeros((2 * count, LANES), jnp.float32)
    period = 2 * total_depth
    for axis in range(2):
        for v in range(VIEWS):
            for s in range(slabs):
                position = d * slabs + s
                num = code_ref[v, axis] * (2 * position + 1 - total_depth)
                w = lax.div(num + 64 * period, period) - 64
                f = (num - w * period).astype(jnp.float32) / float(period)
                here = row_id == axis * count + v * slabs + s
                whole = jnp.where(here, w.astype(jnp.float32), whole)
                frac = jnp.where(here, f, frac)
    lane_f = lax.broadcasted_iota(jnp.int32, (2 * count, LANES), 1).astype(jnp.float32)
    taps = lanczos(frac - (lane_f - float(LANES // 2) - whole))

    lane16 = lax.broadcasted_iota(jnp.int32, (16, LANES), 1)
    row16 = lax.broadcasted_iota(jnp.int32, (16, LANES), 0)
    diagonal = (lane16 - row16) & (LANES - 1)
    zero_tile = jnp.zeros((16, LANES), jnp.bfloat16)

    def column_weights():
        for v in range(VIEWS):
            for s in range(slabs):
                base = take(taps[v * slabs + s : v * slabs + s + 1], diagonal)
                for turn in range(0, LANES, 16):
                    moved = pltpu.roll(base, turn, 1) if turn else base
                    row = v * LANES + turn
                    wx_ref[s, row : row + 16, 0:LANES] = jnp.where(lane16 >= turn, moved, 0.0).astype(jnp.bfloat16)
                    wx_ref[s, row : row + 16, LANES : 2 * LANES] = jnp.where(lane16 < turn, moved, 0.0).astype(jnp.bfloat16)

    turned = band if slots == 1 else 0
    row_base = [MARGIN * turned, MARGIN * (1 - turned)]
    needs_far = [slots == 2, True]
    facing = [jnp.where(code_ref[v, 3] >= 0, 1, 0) for v in range(VIEWS)]

    def slab_at(v, k):
        return jnp.where(facing[v] == 1, slabs - 1 - k, k)

    def row_weights(h):
        view, channel, y = lane16 // (4 * MARGIN), lane16 // MARGIN % 4, lane16 % MARGIN
        for k in range(slabs):
            for v in range(VIEWS):
                at = count + v * slabs
                line = jnp.where(
                    facing[v] == 1, taps[at + slabs - 1 - k : at + slabs - k], taps[at + k : at + k + 1])
                here = v * LANES
                parts = [(r, [[here + c * rows + r] for c in range(4)]) for r in range(0, rows, MARGIN)]
                there = VIEWS * LANES + v * LANES
                if slots == 2:
                    for slot, position in ((0, -MARGIN), (1, rows)):
                        parts.append((position, [[there + (slot * 4 + c) * MARGIN] for c in range(4)]))
                elif needs_far[h]:
                    position = jnp.where(band == 0, rows, -MARGIN)
                    parts.append((position, [[there + (u * 4 + c) * MARGIN for u in range(2)] for c in range(4)]))
                for position, places in parts:
                    tile = take(line, row16 + (position - row_base[h]) - y + LANES // 2)
                    tile = jnp.where(view == v, tile, 0.0)
                    for c in range(4):
                        left = jnp.where(channel == c, tile, 0.0).astype(jnp.bfloat16)
                        right = tile.astype(jnp.bfloat16) if c == 3 else zero_tile
                        for place in places[c]:
                            wy_ref[h, k, place : place + 16, 0:LANES] = left
                            wy_ref[h, k, place : place + 16, LANES : 2 * LANES] = right

    column_weights()

    loads[1].wait()
    for s in range(slabs):
        edge_ref[0, s] = volume_ref[s, rows - MARGIN : rows, :].astype(jnp.float32).astype(jnp.bfloat16)
        edge_ref[1, s] = volume_ref[s, 0:MARGIN, :].astype(jnp.float32).astype(jnp.bfloat16)

    def neighbours(i, n):
        return lax.div(i + n - 1, n) + 1 - lax.div(i + 1, n)

    pl.semaphore_wait(
        barrier, 1 + stations + neighbours(band, band_size))

    units, near_units = extent // LANES, chunk // LANES + 1
    cuts = ((units - near_units, units), (units // 2 - 1, units - near_units), (0, units // 2 - 1))

    def lanes_of(g):
        first, last = cuts[g]
        start = first * low + (units - last) * (1 - low)
        return pl.multiple_of(start * LANES, LANES), last - first

    def group_of(ref, slot, g):
        start, width = lanes_of(g)
        return ref.at[slot, :, :, pl.ds(start, width * LANES)]

    def to_next(g):
        return pltpu.make_async_remote_copy(
            group_of(edge_ref, 0, g), group_of(halo_ref, 0, g), halo_send.at[0, g], halo_recv.at[0, g],
            device_id=(d, lax.rem(band + 1, band_size)), device_id_type=MESH)

    def to_previous(g):
        last = slots - 1
        return pltpu.make_async_remote_copy(
            group_of(edge_ref, 1, g), group_of(halo_ref, last, g), halo_send.at[1, g], halo_recv.at[last, g],
            device_id=(d, lax.rem(band + band_size - 1, band_size)), device_id_type=MESH)

    @pl.when(band < band_size - 1)
    def _():
        for g in range(3):
            to_next(g).start()

    @pl.when(band > 0)
    def _():
        for g in range(3):
            to_previous(g).start()

    loads[2].wait()
    table = tf_ref[...]
    words = table[0:1] | (table[1:2] << 8) | (table[2:3] << 16) | (table[3:4] << 24)
    alpha_unit = 1.0 / (64.0 * total_depth)

    def classify(codes):
        low_bits = codes & (LANES - 1)
        first = take(words[:, 0:LANES], low_bits)
        second = take(words[:, LANES : 2 * LANES], low_bits)
        word = jnp.where(codes >= LANES, second, first)
        alpha = lax.shift_right_logical(word, 24).astype(jnp.float32)
        scaled = alpha * (alpha_unit / 255.0)
        colors = [((word >> shift if shift else word) & 255).astype(jnp.float32) * scaled for shift in (0, 8, 16)]
        return [part.astype(jnp.bfloat16) for part in colors + [alpha * alpha_unit]]

    def own_rows(s, carry):
        for r in range(0, rows, 16):
            for x in range(0, extent, LANES):
                for c, part in enumerate(classify(volume_ref[s, r : r + 16, x : x + LANES])):
                    own_ref[s, c * rows + r : c * rows + r + 16, PAD + x : PAD + x + LANES] = part
        return carry

    lax.fori_loop(0, slabs, own_rows, 0)

    tiles = extent // LANES + 1
    for s in range(slabs):
        for t in range(0, tiles, 2):
            pair = range(t, min(t + 2, tiles))
            data = [own_ref[s, :, u * LANES : (u + 2) * LANES] for u in pair]
            moved = lax.dot_general(
                wx_ref[s], jnp.concatenate(data, axis=0) if len(data) > 1 else data[0],
                (((1,), (1,)), ((), ())), preferred_element_type=jnp.float32).astype(jnp.bfloat16)
            for v in range(VIEWS):
                for i, u in enumerate(pair):
                    moved_ref[v, s, u * LANES : (u + 1) * LANES, 0:LANES] = (
                        moved[v * LANES : (v + 1) * LANES, i * LANES : (i + 1) * LANES])

    for h in range(2):
        row_weights(h)

    has = [band > 0, band < band_size - 1] if slots == 2 else [None]

    def clear(slot):
        row = slot * 4 * MARGIN
        for s in range(slabs):
            far_ref[s, row : row + 4 * MARGIN, PAD : PAD + extent] = jnp.zeros((4 * MARGIN, extent), jnp.bfloat16)

    if slots == 2:
        for slot in range(slots):
            pl.when(jnp.logical_not(has[slot]))(functools.partial(clear, slot))

    def far_rows(g):
        if slots == 1:
            @pl.when(band == 0)
            def _():
                to_next(g).wait()

            @pl.when(band > 0)
            def _():
                to_previous(g).wait()
        else:
            @pl.when(band < band_size - 1)
            def _():
                to_next(g).wait_send()
                to_previous(g).wait_recv()

            @pl.when(band > 0)
            def _():
                to_previous(g).wait_send()
                to_next(g).wait_recv()

        start, width = lanes_of(g)

        def look(slot):
            for s in range(slabs):
                for i in range(width):
                    x = pl.multiple_of(start + i * LANES, LANES)
                    codes = halo_ref[slot, s, :, pl.ds(x, LANES)].astype(jnp.float32).astype(jnp.int32)
                    for c, part in enumerate(classify(codes)):
                        row = slot * 4 * MARGIN + c * MARGIN
                        far_ref[s, row : row + MARGIN, pl.ds(PAD + x, LANES)] = part

        for slot in range(slots):
            if slots == 1:
                look(slot)
            else:
                pl.when(has[slot])(functools.partial(look, slot))

    lane_s = lax.broadcasted_iota(jnp.int32, (piece, LANES), 1)
    first_view = lane_s < LANES // 2
    facing_s = jnp.where(first_view, facing[0], facing[1])

    def over(ahead, near, far):
        front = jnp.where(ahead, near, far)
        back = jnp.where(ahead, far, near)
        return front + (1.0 - replicate_alpha(front, lane_s)) * back

    def first_copy(step, v):
        return pltpu.make_async_remote_copy(
            s1_ref.at[step, v], r1_ref.at[step, v], send1.at[step, v], recv1.at[step, v],
            device_id=at_depth(peer1), device_id_type=MESH)

    def second_copy(step, v):
        return pltpu.make_async_remote_copy(
            s2_ref.at[step, v], r2_ref.at[step, v], send2.at[step, v], recv2.at[step, v],
            device_id=at_depth(peer2), device_id_type=MESH)

    def third_copy(step, v):
        return pltpu.make_async_remote_copy(
            s3_ref.at[step, v], r3_ref.at[z, v], send3.at[step, v], recv3.at[z, v],
            device_id=at_depth(station(step) * 4 + lax.rem(d, 4)), device_id_type=MESH)

    def offset(v, j):
        first = code_ref[v, 2] * (2 * strip * j + 1 - extent) + extent
        shift = lax.div(first + 128 * extent, 2 * extent) - 64
        return jnp.clip(lax.div(shift + 62, 8) * 8 - 64, -MARGIN, 0) + MARGIN

    def strip_of(step, h, q):
        j = station(step) * 4 + q
        at = jnp.where(first_view, offset(0, j), offset(1, j))
        wide = picture_ref[step, h, pl.ds(pl.multiple_of(q * strip, 16), piece + MARGIN), :]
        part = jnp.where(at == 0, wide[0:piece], wide[8 : 8 + piece])
        return jnp.where(at == MARGIN, wide[MARGIN : MARGIN + piece], part)

    near_tiles = chunk // LANES + 1
    lane_t = lax.broadcasted_iota(jnp.int32, (LANES, LANES), 1)

    def far_shear(step):
        start = pl.multiple_of(station(step) * chunk, LANES)
        for s in range(slabs):
            data = [far_ref[s, :, pl.ds(start + t * LANES, 2 * LANES)] for t in range(near_tiles)]
            spare = (-near_tiles * side) % LANES
            if spare:
                data.append(jnp.zeros((spare, 2 * LANES), jnp.bfloat16))
            moved = lax.dot_general(
                wx_ref[s], jnp.concatenate(data, axis=0), (((1,), (1,)), ((), ())), preferred_element_type=jnp.float32)
            for v in range(VIEWS):
                for t in range(near_tiles):
                    at = t * side // LANES * LANES
                    part = moved[v * LANES : (v + 1) * LANES, at : at + LANES]
                    if side < LANES:
                        part = jnp.where(lane_t // side == t * side % LANES // side, part, 0.0)
                    moved_ref[v, s, pl.ds(start + t * LANES, LANES), LANES : 2 * LANES] = part.astype(jnp.bfloat16)

    def render(step, h):
        start = pl.multiple_of(station(step) * chunk + LANES // 2 - MARGIN, 16)
        kinds = 2 if needs_far[h] else 1
        for k in range(slabs):
            data = [
                moved_ref[v, slab_at(v, k), pl.ds(start, reach), kind * LANES : (kind + 1) * LANES]
                for kind in range(kinds) for v in range(VIEWS)]
            sheared_ref[h, k] = jnp.dot(
                jnp.concatenate(data, axis=1), wy_ref[h, k, 0 : kinds * VIEWS * LANES, :],
                preferred_element_type=jnp.float32)
        for q in range(0, reach, 32):
            part = slice(q, q + 32)
            picture = sheared_ref[h, 0, part, 0:LANES]
            for k in range(1, slabs):
                picture = sheared_ref[h, k, part, 0:LANES] + (
                    1.0 - sheared_ref[h, k, part, LANES : 2 * LANES]) * picture
            picture_ref[step, h, part] = picture
        for i in range(2):
            s1_ref[step, h, i] = strip_of(step, h, 2 * i + 1 - core).astype(jnp.bfloat16)
        first_copy(step, h).start()

    def merge1(step, v):
        first_copy(step, v).wait()
        ahead = facing_s == 1 - core
        for h, keep in ((1 - col, False), (col, True)):
            near = strip_of(step, v, 2 * h + core)
            both = over(ahead, near, r1_ref[step, v, h].astype(jnp.float32))
            if keep:
                k2_ref[step, v] = both
            else:
                s2_ref[step, v] = both.astype(jnp.bfloat16)
                second_copy(step, v).start()

    def merge2(step, v):
        second_copy(step, v).wait()
        ahead = facing_s == 1 - col
        both = over(ahead, k2_ref[step, v], r2_ref[step, v].astype(jnp.float32))
        if step == stations - 1:
            mine_ref[v] = both
        else:
            s3_ref[step, v] = both.astype(jnp.bfloat16)
            third_copy(step, v).start()

    def warp_weights(v):
        column = lax.broadcasted_iota(jnp.int32, (strip, piece), 0)
        source = lax.broadcasted_iota(jnp.int32, (strip, piece), 1) + (offset(v, d) - MARGIN)
        double = float(2 * extent)
        column_in = d * strip + source
        inside = jnp.logical_and(column_in >= 0, column_in < extent)
        num = (code_ref[v, 2] * (2 * (d * strip + column) + 1 - extent) + extent).astype(jnp.float32)
        whole_w = jnp.floor(num / double)
        frac_w = (num - whole_w * double) / double
        tap = lanczos(frac_w - ((source - column).astype(jnp.float32) - whole_w))
        return jnp.where(inside, tap, 0.0)

    def far(step):
        if step in (0, 1, half):
            far_rows((0, 1, half).index(step))
        far_shear(step)

    def split(value):
        high = value.astype(jnp.bfloat16)
        return high, (value - high.astype(jnp.float32)).astype(jnp.bfloat16)

    def finish(h, weights):
        for k in range(1, stations):
            other = lax.rem(z + k, stations)
            pltpu.make_async_remote_copy(
                s3_ref.at[0, h], r3_ref.at[other, h], send3.at[0, h], recv3.at[other, h],
                device_id=at_depth(other * 4 + lax.rem(d, 4)), device_id_type=MESH).wait_recv()
        layers = [
            jnp.where(z == k, mine_ref[h], r3_ref[k, h].astype(jnp.float32)) for k in range(stations)]
        picture = None
        for k in range(stations):
            part = jnp.where(facing_s == 1, layers[stations - 1 - k], layers[k])
            if picture is None:
                picture = part
            else:
                picture = part + (1.0 - replicate_alpha(part, lane_s)) * picture
        (wh, wl), (ph, plow) = weights, split(picture)
        final = (
            jnp.dot(wh, ph, preferred_element_type=jnp.float32)
            + jnp.dot(wh, plow, preferred_element_type=jnp.float32)
            + jnp.dot(wl, ph, preferred_element_type=jnp.float32)).T
        for v in range(VIEWS):
            for c in range(4):
                row = (v * 4 + c) * MARGIN
                out_ref[v, pl.ds(pl.multiple_of(c * rows + row_base[h], 8), MARGIN), :] = (
                    final[row : row + MARGIN, v * strip : (v + 1) * strip])

    actions = {
        "far": lambda step, h: far(step),
        "render": render,
        "merge1": merge1,
        "merge2": merge2,
        "warp": lambda step, h: weights.append(split(jnp.concatenate([warp_weights(v) for v in range(VIEWS)], axis=0))),
        "finish": lambda step, h: finish(h, weights[0]),
    }
    weights = []
    for name, step, h in schedule(stations, needs_far[0]):
        actions[name](step, h)
    for step in range(stations - 1):
        for h in range(2):
            third_copy(step, h).wait_send()


def body(volume, tf_table, view_code):
    depth_size, band_size = lax.axis_size("depth"), lax.axis_size("band")
    slabs, rows, extent = volume.shape
    stations = depth_size // 4
    chunk = extent // stations
    strip = chunk // 4
    reach = chunk + 2 * MARGIN
    piece = strip + MARGIN
    slots = 1 if band_size == 2 else 2
    padded = extent + 2 * PAD
    bf16, f32 = jnp.bfloat16, jnp.float32
    vmem, anywhere = pl.BlockSpec(memory_space=pltpu.VMEM), pl.BlockSpec(memory_space=pl.ANY)
    dma = pltpu.SemaphoreType.DMA
    out = pl.pallas_call(
        functools.partial(kernel, (depth_size, band_size)),
        out_shape=jax.ShapeDtypeStruct((VIEWS, LANES, strip), f32),
        in_specs=[anywhere] * 3,
        out_specs=vmem,
        scratch_shapes=[
            pltpu.SMEM(view_code.shape, jnp.int32),
            pltpu.VMEM(volume.shape, jnp.int32),
            pltpu.VMEM(tf_table.shape, jnp.int32),
            pltpu.VMEM((2, slabs, MARGIN, extent), bf16),
            pltpu.VMEM((slots, slabs, MARGIN, extent), bf16),
            pltpu.VMEM((slabs, 4 * rows, padded), bf16),
            pltpu.VMEM((slabs, 4 * MARGIN * slots, padded), bf16),
            pltpu.VMEM((slabs, VIEWS * LANES, 2 * LANES), bf16),
            pltpu.VMEM((2, slabs, 2 * VIEWS * LANES, 2 * LANES), bf16),
            pltpu.VMEM((VIEWS, slabs, extent + LANES, 2 * LANES), bf16),
            pltpu.VMEM((2, slabs, reach, 2 * LANES), f32),
            pltpu.VMEM((stations, VIEWS, reach, LANES), f32),
            pltpu.VMEM((stations, VIEWS, 2, piece, LANES), bf16),
            pltpu.VMEM((stations, VIEWS, 2, piece, LANES), bf16),
            pltpu.VMEM((stations, VIEWS, piece, LANES), bf16),
            pltpu.VMEM((stations, VIEWS, piece, LANES), bf16),
            pltpu.VMEM((stations, VIEWS, piece, LANES), f32),
            pltpu.VMEM((stations, VIEWS, piece, LANES), bf16),
            pltpu.VMEM((stations, VIEWS, piece, LANES), bf16),
            pltpu.VMEM((VIEWS, piece, LANES), f32),
            dma((3,)), dma((2, 3)), dma((slots, 3)),
        ] + [dma((stations, VIEWS))] * 6,
        compiler_params=pltpu.CompilerParams(collective_id=0, has_side_effects=True),
    )(view_code, volume, tf_table)
    return out.reshape(VIEWS, 4, rows, strip).transpose(0, 3, 1, 2)


def solution(mesh):
    P = jax.sharding.PartitionSpec
    placed = (P("depth", "band", None), P(), P())
    return jax.shard_map(
        body, mesh=mesh, in_specs=placed, out_specs=P(None, "depth", None, "band"), check_vma=False
    )
```

```python
import functools

import jax
import jax.numpy as jnp
from jax import lax
from jax.experimental import pallas as pl
from jax.experimental.pallas import tpu as pltpu

VIEWS = 2
MARGIN = 16
PAD = 128
LANES = 128
MESH = pl.DeviceIdType.MESH


def sin_pi(t):
    nearest = jnp.floor(t + 0.5)
    x = jnp.float32(jnp.pi) * (t - nearest)
    odd = nearest - 2.0 * jnp.floor(0.5 * nearest)
    square = x * x
    series = jnp.float32(-1.0 / 39916800.0)
    for factor in (1.0 / 362880.0, -1.0 / 5040.0, 1.0 / 120.0, -1.0 / 6.0, 1.0):
        series = series * square + jnp.float32(factor)
    return x * series * (1.0 - 2.0 * odd)


def lanczos(t):
    safe = jnp.where(t == 0.0, 1.0, t)
    value = sin_pi(t) * sin_pi(t * jnp.float32(1.0 / 3.0)) * jnp.float32(3.0 / jnp.pi**2) / (safe * safe)
    return jnp.where(jnp.abs(t) < 3.0, jnp.where(t == 0.0, 1.0, value), 0.0)


def take(table_row, index):
    table = jnp.broadcast_to(table_row, index.shape)
    return jnp.take_along_axis(table, index, axis=1, mode="promise_in_bounds")


def replicate_alpha(part, lane):
    alpha = jnp.where(lane % (4 * MARGIN) >= 3 * MARGIN, part, 0.0)
    alpha = alpha + pltpu.roll(alpha, LANES - MARGIN, 1)
    return alpha + pltpu.roll(alpha, LANES - 2 * MARGIN, 1)


def schedule(count, early):
    last = count - 1
    order = []
    for i in range(last):
        order += [[("far", i, 0)]] * early + [[("render", i, 0)]]
    for i in range(last):
        order += [[("far", i, 1)]] * (1 - early)
        if i == 0:
            order += [[("merge1", k, 0) for k in range(last)]]
        order += [[("render", i, 1)]]
        if i > 0:
            order += [[("merge1", i - 1, 1)]]
    order += [[("far", last, 0)], [("render", last, 0)], [("merge1", last - 1, 1)] + [("merge2", k, 0) for k in range(last)], [("render", last, 1)]]
    order += [[("merge1", last, 0), ("merge2", 0, 1)]]
    order += [[("merge1", last, 1)] + [("merge2", k, 1) for k in range(1, last - 1)], [("merge2", last - 1, 1)]]
    order += [[("warp", 0, 0)], [("merge2", last, 0)], [("finish", 0, 0)], [("merge2", last, 1)]]
    return order + [[("finish", 0, 1)]]


def kernel(
    sizes, code_hbm, volume_hbm, tf_hbm, out_ref,
    code_ref, volume_ref, tf_ref, edge_ref, halo_ref, own_ref, far_ref, wx_ref, wy_ref, moved_ref, sheared_ref, picture_ref,
    s1_ref, r1_ref, s2_ref, r2_ref, k2_ref, s3_ref, r3_ref, mine_ref,
    load_sem, halo_send, halo_recv, send1, recv1, send2, recv2, send3, recv3,
):
    depth_size, band_size = sizes
    slabs, rows, extent = volume_ref.shape
    stations = depth_size // 4
    chunk = extent // stations
    strip = chunk // 4
    reach = chunk + 2 * MARGIN
    piece = strip + MARGIN
    total_depth = slabs * depth_size
    slots = 1 if band_size == 2 else 2
    side = 4 * MARGIN * slots
    d = lax.axis_index("depth")
    band = lax.axis_index("band")
    core = lax.rem(d, 2)
    col = lax.rem(lax.div(d, 2), 2)
    z = lax.div(d, 4)
    peer1 = d + 1 - 2 * core
    peer2 = d + 2 - 4 * col
    half = stations // 2
    low = 1 - lax.div(z, half)

    def mirrored(i):
        return i * low + (stations - 1 - i) * (1 - low)

    def station(step):
        if step < half:
            return mirrored(stations - 1 - step)
        if step == stations - 1:
            return z
        u, inner = step - half, half - 1 - mirrored(z)
        return mirrored(jnp.where(u < inner, half - 1 - u, u - inner))

    def at_depth(i):
        return (i, band)

    barrier = pltpu.get_barrier_semaphore()

    def greet(device):
        pl.semaphore_signal(barrier, inc=1, device_id=device, device_id_type=MESH)

    @pl.when(band > 0)
    def _():
        greet((d, band - 1))

    @pl.when(band < band_size - 1)
    def _():
        greet((d, band + 1))

    greet(at_depth(peer1))
    greet(at_depth(peer2))
    for k in range(1, stations):
        greet(at_depth(lax.rem(z + k, stations) * 4 + lax.rem(d, 4)))

    loads = [
        pltpu.make_async_copy(source, target, load_sem.at[i])
        for i, (source, target) in enumerate(((code_hbm, code_ref), (volume_hbm, volume_ref), (tf_hbm, tf_ref)))]
    for load in loads:
        load.start()

    for s in range(slabs):
        for ref in (own_ref, far_ref):
            zeros = jnp.zeros((ref.shape[1], PAD), jnp.bfloat16)
            ref[s, :, 0:PAD] = zeros
            ref[s, :, PAD + extent : 2 * PAD + extent] = zeros
    r3_ref[z] = jnp.zeros((VIEWS, piece, LANES), jnp.bfloat16)

    loads[0].wait()
    count = VIEWS * slabs
    row_id = lax.broadcasted_iota(jnp.int32, (2 * count, LANES), 0)
    whole = jnp.zeros((2 * count, LANES), jnp.float32)
    frac = jnp.zeros((2 * count, LANES), jnp.float32)
    period = 2 * total_depth
    for axis in range(2):
        for v in range(VIEWS):
            for s in range(slabs):
                position = d * slabs + s
                num = code_ref[v, axis] * (2 * position + 1 - total_depth)
                w = lax.div(num + 64 * period, period) - 64
                f = (num - w * period).astype(jnp.float32) / float(period)
                here = row_id == axis * count + v * slabs + s
                whole = jnp.where(here, w.astype(jnp.float32), whole)
                frac = jnp.where(here, f, frac)
    lane_f = lax.broadcasted_iota(jnp.int32, (2 * count, LANES), 1).astype(jnp.float32)
    taps = lanczos(frac - (lane_f - float(LANES // 2) - whole))

    lane16 = lax.broadcasted_iota(jnp.int32, (16, LANES), 1)
    row16 = lax.broadcasted_iota(jnp.int32, (16, LANES), 0)
    diagonal = (lane16 - row16) & (LANES - 1)
    zero_tile = jnp.zeros((16, LANES), jnp.bfloat16)

    def column_weights():
        for v in range(VIEWS):
            for s in range(slabs):
                base = take(taps[v * slabs + s : v * slabs + s + 1], diagonal)
                for turn in range(0, LANES, 16):
                    moved = pltpu.roll(base, turn, 1) if turn else base
                    row = v * LANES + turn
                    wx_ref[s, row : row + 16, 0:LANES] = jnp.where(lane16 >= turn, moved, 0.0).astype(jnp.bfloat16)
                    wx_ref[s, row : row + 16, LANES : 2 * LANES] = jnp.where(lane16 < turn, moved, 0.0).astype(jnp.bfloat16)

    turned = band if slots == 1 else 0
    row_base = [MARGIN * turned, MARGIN * (1 - turned)]
    needs_far = [slots == 2, True]
    facing = [jnp.where(code_ref[v, 3] >= 0, 1, 0) for v in range(VIEWS)]

    def slab_at(v, k):
        return jnp.where(facing[v] == 1, slabs - 1 - k, k)

    def row_weights(h):
        view, channel, y = lane16 // (4 * MARGIN), lane16 // MARGIN % 4, lane16 % MARGIN
        for k in range(slabs):
            for v in range(VIEWS):
                at = count + v * slabs
                line = jnp.where(
                    facing[v] == 1, taps[at + slabs - 1 - k : at + slabs - k], taps[at + k : at + k + 1])
                here = v * LANES
                parts = [(r, [[here + c * rows + r] for c in range(4)]) for r in range(0, rows, MARGIN)]
                there = VIEWS * LANES + v * LANES
                if slots == 2:
                    for slot, position in ((0, -MARGIN), (1, rows)):
                        parts.append((position, [[there + (slot * 4 + c) * MARGIN] for c in range(4)]))
                elif needs_far[h]:
                    position = jnp.where(band == 0, rows, -MARGIN)
                    parts.append((position, [[there + (u * 4 + c) * MARGIN for u in range(2)] for c in range(4)]))
                for position, places in parts:
                    tile = take(line, row16 + (position - row_base[h]) - y + LANES // 2)
                    tile = jnp.where(view == v, tile, 0.0)
                    for c in range(4):
                        left = jnp.where(channel == c, tile, 0.0).astype(jnp.bfloat16)
                        right = tile.astype(jnp.bfloat16) if c == 3 else zero_tile
                        for place in places[c]:
                            wy_ref[h, k, place : place + 16, 0:LANES] = left
                            wy_ref[h, k, place : place + 16, LANES : 2 * LANES] = right

    column_weights()

    loads[1].wait()
    for s in range(slabs):
        edge_ref[0, s] = volume_ref[s, rows - MARGIN : rows, :].astype(jnp.float32).astype(jnp.bfloat16)
        edge_ref[1, s] = volume_ref[s, 0:MARGIN, :].astype(jnp.float32).astype(jnp.bfloat16)

    def neighbours(i, n):
        return lax.div(i + n - 1, n) + 1 - lax.div(i + 1, n)

    pl.semaphore_wait(
        barrier, 1 + stations + neighbours(band, band_size))

    units, near_units = extent // LANES, chunk // LANES + 1
    cuts = ((units - near_units, units), (units // 2 - 1, units - near_units), (0, units // 2 - 1))

    def lanes_of(g):
        first, last = cuts[g]
        start = first * low + (units - last) * (1 - low)
        return pl.multiple_of(start * LANES, LANES), last - first

    def group_of(ref, slot, g):
        start, width = lanes_of(g)
        return ref.at[slot, :, :, pl.ds(start, width * LANES)]

    def to_next(g):
        return pltpu.make_async_remote_copy(
            group_of(edge_ref, 0, g), group_of(halo_ref, 0, g), halo_send.at[0, g], halo_recv.at[0, g],
            device_id=(d, lax.rem(band + 1, band_size)), device_id_type=MESH)

    def to_previous(g):
        last = slots - 1
        return pltpu.make_async_remote_copy(
            group_of(edge_ref, 1, g), group_of(halo_ref, last, g), halo_send.at[1, g], halo_recv.at[last, g],
            device_id=(d, lax.rem(band + band_size - 1, band_size)), device_id_type=MESH)

    @pl.when(band < band_size - 1)
    def _():
        for g in range(3):
            to_next(g).start()

    @pl.when(band > 0)
    def _():
        for g in range(3):
            to_previous(g).start()

    loads[2].wait()
    table = tf_ref[...]
    words = table[0:1] | (table[1:2] << 8) | (table[2:3] << 16) | (table[3:4] << 24)
    alpha_unit = 1.0 / (64.0 * total_depth)

    def classify(codes):
        low_bits = codes & (LANES - 1)
        first = take(words[:, 0:LANES], low_bits)
        second = take(words[:, LANES : 2 * LANES], low_bits)
        word = jnp.where(codes >= LANES, second, first)
        alpha = lax.shift_right_logical(word, 24).astype(jnp.float32)
        scaled = alpha * (alpha_unit / 255.0)
        colors = [((word >> shift if shift else word) & 255).astype(jnp.float32) * scaled for shift in (0, 8, 16)]
        return [part.astype(jnp.bfloat16) for part in colors + [alpha * alpha_unit]]

    def own_rows(s, carry):
        for r in range(0, rows, 16):
            for x in range(0, extent, LANES):
                for c, part in enumerate(classify(volume_ref[s, r : r + 16, x : x + LANES])):
                    own_ref[s, c * rows + r : c * rows + r + 16, PAD + x : PAD + x + LANES] = part
        return carry

    lax.fori_loop(0, slabs, own_rows, 0)

    tiles = extent // LANES + 1
    for s in range(slabs):
        for t in range(0, tiles, 2):
            pair = range(t, min(t + 2, tiles))
            data = [own_ref[s, :, u * LANES : (u + 2) * LANES] for u in pair]
            moved = lax.dot_general(
                wx_ref[s], jnp.concatenate(data, axis=0) if len(data) > 1 else data[0],
                (((1,), (1,)), ((), ())), preferred_element_type=jnp.float32).astype(jnp.bfloat16)
            for v in range(VIEWS):
                for i, u in enumerate(pair):
                    moved_ref[v, s, u * LANES : (u + 1) * LANES, 0:LANES] = (
                        moved[v * LANES : (v + 1) * LANES, i * LANES : (i + 1) * LANES])

    for h in range(2):
        row_weights(h)

    has = [band > 0, band < band_size - 1] if slots == 2 else [None]

    def clear(slot):
        row = slot * 4 * MARGIN
        for s in range(slabs):
            far_ref[s, row : row + 4 * MARGIN, PAD : PAD + extent] = jnp.zeros((4 * MARGIN, extent), jnp.bfloat16)

    if slots == 2:
        for slot in range(slots):
            pl.when(jnp.logical_not(has[slot]))(functools.partial(clear, slot))

    def far_rows(g):
        if slots == 1:
            @pl.when(band == 0)
            def _():
                to_next(g).wait()

            @pl.when(band > 0)
            def _():
                to_previous(g).wait()
        else:
            @pl.when(band < band_size - 1)
            def _():
                to_next(g).wait_send()
                to_previous(g).wait_recv()

            @pl.when(band > 0)
            def _():
                to_previous(g).wait_send()
                to_next(g).wait_recv()

        start, width = lanes_of(g)

        def look(slot):
            for s in range(slabs):
                for i in range(width):
                    x = pl.multiple_of(start + i * LANES, LANES)
                    codes = halo_ref[slot, s, :, pl.ds(x, LANES)].astype(jnp.float32).astype(jnp.int32)
                    for c, part in enumerate(classify(codes)):
                        row = slot * 4 * MARGIN + c * MARGIN
                        far_ref[s, row : row + MARGIN, pl.ds(PAD + x, LANES)] = part

        for slot in range(slots):
            if slots == 1:
                look(slot)
            else:
                pl.when(has[slot])(functools.partial(look, slot))

    lane_s = lax.broadcasted_iota(jnp.int32, (piece, LANES), 1)
    first_view = lane_s < LANES // 2
    facing_s = jnp.where(first_view, facing[0], facing[1])

    def over(ahead, near, far):
        front = jnp.where(ahead, near, far)
        back = jnp.where(ahead, far, near)
        return front + (1.0 - replicate_alpha(front, lane_s)) * back

    def first_copy(step, v):
        return pltpu.make_async_remote_copy(
            s1_ref.at[step, v], r1_ref.at[step, v], send1.at[step, v], recv1.at[step, v],
            device_id=at_depth(peer1), device_id_type=MESH)

    def second_copy(step, v):
        return pltpu.make_async_remote_copy(
            s2_ref.at[step, v], r2_ref.at[step, v], send2.at[step, v], recv2.at[step, v],
            device_id=at_depth(peer2), device_id_type=MESH)

    def third_copy(step, v):
        return pltpu.make_async_remote_copy(
            s3_ref.at[step, v], r3_ref.at[z, v], send3.at[step, v], recv3.at[z, v],
            device_id=at_depth(station(step) * 4 + lax.rem(d, 4)), device_id_type=MESH)

    def offset(v, j):
        first = code_ref[v, 2] * (2 * strip * j + 1 - extent) + extent
        shift = lax.div(first + 128 * extent, 2 * extent) - 64
        return jnp.clip(lax.div(shift + 62, 8) * 8 - 64, -MARGIN, 0) + MARGIN

    def strip_of(step, h, q):
        j = station(step) * 4 + q
        at = jnp.where(first_view, offset(0, j), offset(1, j))
        wide = picture_ref[step, h, pl.ds(pl.multiple_of(q * strip, 16), piece + MARGIN), :]
        part = jnp.where(at == 0, wide[0:piece], wide[8 : 8 + piece])
        return jnp.where(at == MARGIN, wide[MARGIN : MARGIN + piece], part)

    near_tiles = chunk // LANES + 1
    lane_t = lax.broadcasted_iota(jnp.int32, (LANES, LANES), 1)

    def far_shear(step):
        start = pl.multiple_of(station(step) * chunk, LANES)
        for s in range(slabs):
            data = [far_ref[s, :, pl.ds(start + t * LANES, 2 * LANES)] for t in range(near_tiles)]
            spare = (-near_tiles * side) % LANES
            if spare:
                data.append(jnp.zeros((spare, 2 * LANES), jnp.bfloat16))
            moved = lax.dot_general(
                wx_ref[s], jnp.concatenate(data, axis=0), (((1,), (1,)), ((), ())), preferred_element_type=jnp.float32)
            for v in range(VIEWS):
                for t in range(near_tiles):
                    at = t * side // LANES * LANES
                    part = moved[v * LANES : (v + 1) * LANES, at : at + LANES]
                    if side < LANES:
                        part = jnp.where(lane_t // side == t * side % LANES // side, part, 0.0)
                    moved_ref[v, s, pl.ds(start + t * LANES, LANES), LANES : 2 * LANES] = part.astype(jnp.bfloat16)

    def render(step, h):
        start = pl.multiple_of(station(step) * chunk + LANES // 2 - MARGIN, 16)
        kinds = 2 if needs_far[h] else 1
        for k in range(slabs):
            data = [
                moved_ref[v, slab_at(v, k), pl.ds(start, reach), kind * LANES : (kind + 1) * LANES]
                for kind in range(kinds) for v in range(VIEWS)]
            sheared_ref[h, k] = jnp.dot(
                jnp.concatenate(data, axis=1), wy_ref[h, k, 0 : kinds * VIEWS * LANES, :],
                preferred_element_type=jnp.float32)
        for q in range(0, reach, 32):
            part = slice(q, q + 32)
            picture = sheared_ref[h, 0, part, 0:LANES]
            for k in range(1, slabs):
                picture = sheared_ref[h, k, part, 0:LANES] + (
                    1.0 - sheared_ref[h, k, part, LANES : 2 * LANES]) * picture
            picture_ref[step, h, part] = picture
        for i in range(2):
            s1_ref[step, h, i] = strip_of(step, h, 2 * i + 1 - core).astype(jnp.bfloat16)
        first_copy(step, h).start()

    def merge1(step, h):
        ahead = facing_s == 1 - core
        for q, keep in ((1 - col, False), (col, True)):
            near = strip_of(step, h, 2 * q + core)
            both = over(ahead, near, r1_ref[step, h, q].astype(jnp.float32))
            if keep:
                k2_ref[step, h] = both
            else:
                s2_ref[step, h] = both.astype(jnp.bfloat16)

    def merge2(step, h):
        ahead = facing_s == 1 - col
        both = over(ahead, k2_ref[step, h], r2_ref[step, h].astype(jnp.float32))
        if step == stations - 1:
            mine_ref[h] = both
        else:
            s3_ref[step, h] = both.astype(jnp.bfloat16)

    def merges(parts):
        for name, step, h in parts:
            (first_copy if name == "merge1" else second_copy)(step, h).wait()
        for name, step, h in parts:
            (merge1 if name == "merge1" else merge2)(step, h)
        for name, step, h in parts:
            if name == "merge1":
                second_copy(step, h).start()
            elif step < stations - 1:
                third_copy(step, h).start()

    def warp_weights(v):
        column = lax.broadcasted_iota(jnp.int32, (strip, piece), 0)
        source = lax.broadcasted_iota(jnp.int32, (strip, piece), 1) + (offset(v, d) - MARGIN)
        double = float(2 * extent)
        column_in = d * strip + source
        inside = jnp.logical_and(column_in >= 0, column_in < extent)
        num = (code_ref[v, 2] * (2 * (d * strip + column) + 1 - extent) + extent).astype(jnp.float32)
        whole_w = jnp.floor(num / double)
        frac_w = (num - whole_w * double) / double
        tap = lanczos(frac_w - ((source - column).astype(jnp.float32) - whole_w))
        return jnp.where(inside, tap, 0.0)

    def far(step):
        if step in (0, 1, half):
            far_rows((0, 1, half).index(step))
        far_shear(step)

    def split(value):
        high = value.astype(jnp.bfloat16)
        return high, (value - high.astype(jnp.float32)).astype(jnp.bfloat16)

    def finish(h, weights):
        for k in range(1, stations):
            other = lax.rem(z + k, stations)
            pltpu.make_async_remote_copy(
                s3_ref.at[0, h], r3_ref.at[other, h], send3.at[0, h], recv3.at[other, h],
                device_id=at_depth(other * 4 + lax.rem(d, 4)), device_id_type=MESH).wait_recv()
        layers = [
            jnp.where(z == k, mine_ref[h], r3_ref[k, h].astype(jnp.float32)) for k in range(stations)]
        picture = None
        for k in range(stations):
            part = jnp.where(facing_s == 1, layers[stations - 1 - k], layers[k])
            if picture is None:
                picture = part
            else:
                picture = part + (1.0 - replicate_alpha(part, lane_s)) * picture
        (wh, wl), (ph, plow) = weights, split(picture)
        crossed = (((0,), (1,)), ((), ()))
        final = (
            lax.dot_general(ph, wh, crossed, preferred_element_type=jnp.float32)
            + lax.dot_general(plow, wh, crossed, preferred_element_type=jnp.float32)
            + lax.dot_general(ph, wl, crossed, preferred_element_type=jnp.float32))
        for v in range(VIEWS):
            for c in range(4):
                row = (v * 4 + c) * MARGIN
                out_ref[v, pl.ds(pl.multiple_of(c * rows + row_base[h], 8), MARGIN), :] = (
                    final[row : row + MARGIN, v * strip : (v + 1) * strip])

    actions = {
        "far": lambda step, h: far(step),
        "render": render,
        "warp": lambda step, h: weights.append(split(jnp.concatenate([warp_weights(v) for v in range(VIEWS)], axis=0))),
        "finish": lambda step, h: finish(h, weights[0]),
    }
    weights = []
    for group in schedule(stations, needs_far[0]):
        if group[0][0] in actions:
            for name, step, h in group:
                actions[name](step, h)
        else:
            merges(group)
    for step in range(stations - 1):
        for h in range(2):
            third_copy(step, h).wait_send()


def body(volume, tf_table, view_code):
    depth_size, band_size = lax.axis_size("depth"), lax.axis_size("band")
    slabs, rows, extent = volume.shape
    stations = depth_size // 4
    chunk = extent // stations
    strip = chunk // 4
    reach = chunk + 2 * MARGIN
    piece = strip + MARGIN
    slots = 1 if band_size == 2 else 2
    padded = extent + 2 * PAD
    bf16, f32 = jnp.bfloat16, jnp.float32
    vmem, anywhere = pl.BlockSpec(memory_space=pltpu.VMEM), pl.BlockSpec(memory_space=pl.ANY)
    dma = pltpu.SemaphoreType.DMA
    out = pl.pallas_call(
        functools.partial(kernel, (depth_size, band_size)),
        out_shape=jax.ShapeDtypeStruct((VIEWS, LANES, strip), f32),
        in_specs=[anywhere] * 3,
        out_specs=vmem,
        scratch_shapes=[
            pltpu.SMEM(view_code.shape, jnp.int32),
            pltpu.VMEM(volume.shape, jnp.int32),
            pltpu.VMEM(tf_table.shape, jnp.int32),
            pltpu.VMEM((2, slabs, MARGIN, extent), bf16),
            pltpu.VMEM((slots, slabs, MARGIN, extent), bf16),
            pltpu.VMEM((slabs, 4 * rows, padded), bf16),
            pltpu.VMEM((slabs, 4 * MARGIN * slots, padded), bf16),
            pltpu.VMEM((slabs, VIEWS * LANES, 2 * LANES), bf16),
            pltpu.VMEM((2, slabs, 2 * VIEWS * LANES, 2 * LANES), bf16),
            pltpu.VMEM((VIEWS, slabs, extent + LANES, 2 * LANES), bf16),
            pltpu.VMEM((2, slabs, reach, 2 * LANES), f32),
            pltpu.VMEM((stations, VIEWS, reach, LANES), f32),
            pltpu.VMEM((stations, VIEWS, 2, piece, LANES), bf16),
            pltpu.VMEM((stations, VIEWS, 2, piece, LANES), bf16),
            pltpu.VMEM((stations, VIEWS, piece, LANES), bf16),
            pltpu.VMEM((stations, VIEWS, piece, LANES), bf16),
            pltpu.VMEM((stations, VIEWS, piece, LANES), f32),
            pltpu.VMEM((stations, VIEWS, piece, LANES), bf16),
            pltpu.VMEM((stations, VIEWS, piece, LANES), bf16),
            pltpu.VMEM((VIEWS, piece, LANES), f32),
            dma((3,)), dma((2, 3)), dma((slots, 3)),
        ] + [dma((stations, VIEWS))] * 6,
        compiler_params=pltpu.CompilerParams(collective_id=0, has_side_effects=True),
    )(view_code, volume, tf_table)
    return out.reshape(VIEWS, 4, rows, strip).transpose(0, 3, 1, 2)


def solution(mesh):
    P = jax.sharding.PartitionSpec
    placed = (P("depth", "band", None), P(), P())
    return jax.shard_map(
        body, mesh=mesh, in_specs=placed, out_specs=P(None, "depth", None, "band"), check_vma=False
    )
```

```python
import functools

import jax
import jax.numpy as jnp
from jax import lax
from jax.experimental import pallas as pl
from jax.experimental.pallas import tpu as pltpu

VIEWS = 2
MARGIN = 16
PAD = 128
LANES = 128
MESH = pl.DeviceIdType.MESH


def sin_pi(t):
    nearest = jnp.floor(t + 0.5)
    x = jnp.float32(jnp.pi) * (t - nearest)
    odd = nearest - 2.0 * jnp.floor(0.5 * nearest)
    square = x * x
    series = jnp.float32(-1.0 / 39916800.0)
    for factor in (1.0 / 362880.0, -1.0 / 5040.0, 1.0 / 120.0, -1.0 / 6.0, 1.0):
        series = series * square + jnp.float32(factor)
    return x * series * (1.0 - 2.0 * odd)


def lanczos(t):
    safe = jnp.where(t == 0.0, 1.0, t)
    value = sin_pi(t) * sin_pi(t * jnp.float32(1.0 / 3.0)) * jnp.float32(3.0 / jnp.pi**2) / (safe * safe)
    return jnp.where(jnp.abs(t) < 3.0, jnp.where(t == 0.0, 1.0, value), 0.0)


def split(value):
    high = value.astype(jnp.bfloat16)
    return high, (value - high.astype(jnp.float32)).astype(jnp.bfloat16)


def take(table_row, index):
    table = jnp.broadcast_to(table_row, index.shape)
    return jnp.take_along_axis(table, index, axis=1, mode="promise_in_bounds")


def replicate_alpha(part, lane):
    alpha = jnp.where(lane % (4 * MARGIN) >= 3 * MARGIN, part, 0.0)
    alpha = alpha + pltpu.roll(alpha, LANES - MARGIN, 1)
    return alpha + pltpu.roll(alpha, LANES - 2 * MARGIN, 1)


def schedule(count, early):
    last = count - 1
    order = []
    for i in range(last):
        order += [[("far", i, 0)]] * early + [[("render", i, 0)]]
    for i in range(last):
        order += [[("far", i, 1)]] * (1 - early)
        if i == 0:
            order += [[("merge1", k, 0) for k in range(last)]]
        order += [[("render", i, 1)]]
        if i > 0:
            order += [[("merge1", i - 1, 1)] + [("merge2", 0, 0)] * (i == last - 1)]
    order += [[("far", last, 0)], [("render", last, 0)], [("merge1", last - 1, 1)] + [("merge2", k, 0) for k in range(1, last)], [("render", last, 1)]]
    order += [[("merge1", last, 0), ("merge2", 0, 1)]]
    order += [[("merge1", last, 1)] + [("merge2", k, 1) for k in range(1, last - 1)], [("merge2", last - 1, 1)]]
    order += [[("warp", 0, 0)], [("merge2", last, 0)], [("finish", 0, 0)], [("merge2", last, 1)]]
    return order + [[("finish", 0, 1)]]


def kernel(
    sizes, code_hbm, volume_hbm, tf_hbm, composite_ref, weights_ref,
    code_ref, volume_ref, tf_ref, edge_ref, halo_ref, own_ref, far_ref, wx_ref, wy_ref, moved_ref, sheared_ref, picture_ref,
    s1_ref, r1_ref, s2_ref, r2_ref, k2_ref, s3_ref, r3_ref, mine_ref,
    load_sem, halo_send, halo_recv, send1, recv1, send2, recv2, send3, recv3,
):
    depth_size, band_size = sizes
    slabs, rows, extent = volume_ref.shape
    stations = depth_size // 4
    chunk = extent // stations
    strip = chunk // 4
    reach = chunk + 2 * MARGIN
    piece = strip + MARGIN
    total_depth = slabs * depth_size
    slots = 1 if band_size == 2 else 2
    side = 4 * MARGIN * slots
    d = lax.axis_index("depth")
    band = lax.axis_index("band")
    core = lax.rem(d, 2)
    col = lax.rem(lax.div(d, 2), 2)
    z = lax.div(d, 4)
    peer1 = d + 1 - 2 * core
    peer2 = d + 2 - 4 * col
    half = stations // 2
    low = 1 - lax.div(z, half)

    def mirrored(i):
        return i * low + (stations - 1 - i) * (1 - low)

    def station(step):
        if step < half:
            return mirrored(stations - 1 - step)
        if step == stations - 1:
            return z
        u, inner = step - half, half - 1 - mirrored(z)
        return mirrored(jnp.where(u < inner, half - 1 - u, u - inner))

    def at_depth(i):
        return (i, band)

    barrier = pltpu.get_barrier_semaphore()

    def greet(device):
        pl.semaphore_signal(barrier, inc=1, device_id=device, device_id_type=MESH)

    @pl.when(band > 0)
    def _():
        greet((d, band - 1))

    @pl.when(band < band_size - 1)
    def _():
        greet((d, band + 1))

    greet(at_depth(peer1))
    greet(at_depth(peer2))
    for k in range(1, stations):
        greet(at_depth(lax.rem(z + k, stations) * 4 + lax.rem(d, 4)))

    loads = [
        pltpu.make_async_copy(source, target, load_sem.at[i])
        for i, (source, target) in enumerate(((code_hbm, code_ref), (volume_hbm, volume_ref), (tf_hbm, tf_ref)))]
    for load in loads:
        load.start()

    for s in range(slabs):
        for ref in (own_ref, far_ref):
            zeros = jnp.zeros((ref.shape[1], PAD), jnp.bfloat16)
            ref[s, :, 0:PAD] = zeros
            ref[s, :, PAD + extent : 2 * PAD + extent] = zeros
    r3_ref[z] = jnp.zeros((VIEWS, piece, LANES), jnp.bfloat16)

    loads[0].wait()
    count = VIEWS * slabs
    row_id = lax.broadcasted_iota(jnp.int32, (2 * count, LANES), 0)
    whole = jnp.zeros((2 * count, LANES), jnp.float32)
    frac = jnp.zeros((2 * count, LANES), jnp.float32)
    period = 2 * total_depth
    for axis in range(2):
        for v in range(VIEWS):
            for s in range(slabs):
                position = d * slabs + s
                num = code_ref[v, axis] * (2 * position + 1 - total_depth)
                w = lax.div(num + 64 * period, period) - 64
                f = (num - w * period).astype(jnp.float32) / float(period)
                here = row_id == axis * count + v * slabs + s
                whole = jnp.where(here, w.astype(jnp.float32), whole)
                frac = jnp.where(here, f, frac)
    lane_f = lax.broadcasted_iota(jnp.int32, (2 * count, LANES), 1).astype(jnp.float32)
    taps = lanczos(frac - (lane_f - float(LANES // 2) - whole))

    lane16 = lax.broadcasted_iota(jnp.int32, (16, LANES), 1)
    row16 = lax.broadcasted_iota(jnp.int32, (16, LANES), 0)
    diagonal = (lane16 - row16) & (LANES - 1)
    zero_tile = jnp.zeros((16, LANES), jnp.bfloat16)

    def column_weights():
        for v in range(VIEWS):
            for s in range(slabs):
                base = take(taps[v * slabs + s : v * slabs + s + 1], diagonal)
                for turn in range(0, LANES, 16):
                    moved = pltpu.roll(base, turn, 1) if turn else base
                    row = v * LANES + turn
                    wx_ref[s, row : row + 16, 0:LANES] = jnp.where(lane16 >= turn, moved, 0.0).astype(jnp.bfloat16)
                    wx_ref[s, row : row + 16, LANES : 2 * LANES] = jnp.where(lane16 < turn, moved, 0.0).astype(jnp.bfloat16)

    turned = band if slots == 1 else 0
    row_base = [MARGIN * turned, MARGIN * (1 - turned)]
    needs_far = [slots == 2, True]
    facing = [jnp.where(code_ref[v, 3] >= 0, 1, 0) for v in range(VIEWS)]

    def slab_at(v, k):
        return jnp.where(facing[v] == 1, slabs - 1 - k, k)

    def row_weights(h):
        view, channel, y = lane16 // (4 * MARGIN), lane16 // MARGIN % 4, lane16 % MARGIN
        for k in range(slabs):
            for v in range(VIEWS):
                at = count + v * slabs
                line = jnp.where(
                    facing[v] == 1, taps[at + slabs - 1 - k : at + slabs - k], taps[at + k : at + k + 1])
                here = v * LANES
                parts = [(r, [[here + c * rows + r] for c in range(4)]) for r in range(0, rows, MARGIN)]
                there = VIEWS * LANES + v * LANES
                if slots == 2:
                    for slot, position in ((0, -MARGIN), (1, rows)):
                        parts.append((position, [[there + (slot * 4 + c) * MARGIN] for c in range(4)]))
                elif needs_far[h]:
                    position = jnp.where(band == 0, rows, -MARGIN)
                    parts.append((position, [[there + (u * 4 + c) * MARGIN for u in range(2)] for c in range(4)]))
                for position, places in parts:
                    tile = take(line, row16 + (position - row_base[h]) - y + LANES // 2)
                    tile = jnp.where(view == v, tile, 0.0)
                    for c in range(4):
                        left = jnp.where(channel == c, tile, 0.0).astype(jnp.bfloat16)
                        right = tile.astype(jnp.bfloat16) if c == 3 else zero_tile
                        for place in places[c]:
                            wy_ref[h, k, place : place + 16, 0:LANES] = left
                            wy_ref[h, k, place : place + 16, LANES : 2 * LANES] = right

    column_weights()

    loads[1].wait()
    for s in range(slabs):
        edge_ref[0, s] = volume_ref[s, rows - MARGIN : rows, :].astype(jnp.float32).astype(jnp.bfloat16)
        edge_ref[1, s] = volume_ref[s, 0:MARGIN, :].astype(jnp.float32).astype(jnp.bfloat16)

    def neighbours(i, n):
        return lax.div(i + n - 1, n) + 1 - lax.div(i + 1, n)

    pl.semaphore_wait(
        barrier, 1 + stations + neighbours(band, band_size))

    units, near_units = extent // LANES, chunk // LANES + 1
    cuts = ((units - near_units, units), (units // 2 - 1, units - near_units), (0, units // 2 - 1))

    def lanes_of(g):
        first, last = cuts[g]
        start = first * low + (units - last) * (1 - low)
        return pl.multiple_of(start * LANES, LANES), last - first

    def group_of(ref, slot, g):
        start, width = lanes_of(g)
        return ref.at[slot, :, :, pl.ds(start, width * LANES)]

    def to_next(g):
        return pltpu.make_async_remote_copy(
            group_of(edge_ref, 0, g), group_of(halo_ref, 0, g), halo_send.at[0, g], halo_recv.at[0, g],
            device_id=(d, lax.rem(band + 1, band_size)), device_id_type=MESH)

    def to_previous(g):
        last = slots - 1
        return pltpu.make_async_remote_copy(
            group_of(edge_ref, 1, g), group_of(halo_ref, last, g), halo_send.at[1, g], halo_recv.at[last, g],
            device_id=(d, lax.rem(band + band_size - 1, band_size)), device_id_type=MESH)

    @pl.when(band < band_size - 1)
    def _():
        for g in range(3):
            to_next(g).start()

    @pl.when(band > 0)
    def _():
        for g in range(3):
            to_previous(g).start()

    loads[2].wait()
    table = tf_ref[...]
    words = table[0:1] | (table[1:2] << 8) | (table[2:3] << 16) | (table[3:4] << 24)
    alpha_unit = 1.0 / (64.0 * total_depth)

    def classify(codes):
        low_bits = codes & (LANES - 1)
        first = take(words[:, 0:LANES], low_bits)
        second = take(words[:, LANES : 2 * LANES], low_bits)
        word = jnp.where(codes >= LANES, second, first)
        alpha = lax.shift_right_logical(word, 24).astype(jnp.float32)
        scaled = alpha * (alpha_unit / 255.0)
        colors = [((word >> shift if shift else word) & 255).astype(jnp.float32) * scaled for shift in (0, 8, 16)]
        return [part.astype(jnp.bfloat16) for part in colors + [alpha * alpha_unit]]

    def own_rows(s, carry):
        for r in range(0, rows, 16):
            for x in range(0, extent, LANES):
                for c, part in enumerate(classify(volume_ref[s, r : r + 16, x : x + LANES])):
                    own_ref[s, c * rows + r : c * rows + r + 16, PAD + x : PAD + x + LANES] = part
        return carry

    lax.fori_loop(0, slabs, own_rows, 0)

    tiles = extent // LANES + 1
    for s in range(slabs):
        for t in range(0, tiles, 2):
            pair = range(t, min(t + 2, tiles))
            data = [own_ref[s, :, u * LANES : (u + 2) * LANES] for u in pair]
            moved = lax.dot_general(
                wx_ref[s], jnp.concatenate(data, axis=0) if len(data) > 1 else data[0],
                (((1,), (1,)), ((), ())), preferred_element_type=jnp.float32).astype(jnp.bfloat16)
            for v in range(VIEWS):
                for i, u in enumerate(pair):
                    moved_ref[v, s, u * LANES : (u + 1) * LANES, 0:LANES] = (
                        moved[v * LANES : (v + 1) * LANES, i * LANES : (i + 1) * LANES])

    for h in range(2):
        row_weights(h)

    has = [band > 0, band < band_size - 1] if slots == 2 else [None]

    def clear(slot):
        row = slot * 4 * MARGIN
        for s in range(slabs):
            far_ref[s, row : row + 4 * MARGIN, PAD : PAD + extent] = jnp.zeros((4 * MARGIN, extent), jnp.bfloat16)

    if slots == 2:
        for slot in range(slots):
            pl.when(jnp.logical_not(has[slot]))(functools.partial(clear, slot))

    def far_rows(g):
        if slots == 1:
            @pl.when(band == 0)
            def _():
                to_next(g).wait()

            @pl.when(band > 0)
            def _():
                to_previous(g).wait()
        else:
            @pl.when(band < band_size - 1)
            def _():
                to_next(g).wait_send()
                to_previous(g).wait_recv()

            @pl.when(band > 0)
            def _():
                to_previous(g).wait_send()
                to_next(g).wait_recv()

        start, width = lanes_of(g)

        def look(slot):
            for s in range(slabs):
                for i in range(width):
                    x = pl.multiple_of(start + i * LANES, LANES)
                    codes = halo_ref[slot, s, :, pl.ds(x, LANES)].astype(jnp.float32).astype(jnp.int32)
                    for c, part in enumerate(classify(codes)):
                        row = slot * 4 * MARGIN + c * MARGIN
                        far_ref[s, row : row + MARGIN, pl.ds(PAD + x, LANES)] = part

        for slot in range(slots):
            if slots == 1:
                look(slot)
            else:
                pl.when(has[slot])(functools.partial(look, slot))

    lane_s = lax.broadcasted_iota(jnp.int32, (piece, LANES), 1)
    first_view = lane_s < LANES // 2
    facing_s = jnp.where(first_view, facing[0], facing[1])

    def over(ahead, near, far):
        front = jnp.where(ahead, near, far)
        back = jnp.where(ahead, far, near)
        return front + (1.0 - replicate_alpha(front, lane_s)) * back

    def first_copy(step, v):
        return pltpu.make_async_remote_copy(
            s1_ref.at[step, v], r1_ref.at[step, v], send1.at[step, v], recv1.at[step, v],
            device_id=at_depth(peer1), device_id_type=MESH)

    def second_copy(step, v):
        return pltpu.make_async_remote_copy(
            s2_ref.at[step, v], r2_ref.at[step, v], send2.at[step, v], recv2.at[step, v],
            device_id=at_depth(peer2), device_id_type=MESH)

    def third_copy(step, v):
        return pltpu.make_async_remote_copy(
            s3_ref.at[step, v], r3_ref.at[z, v], send3.at[step, v], recv3.at[z, v],
            device_id=at_depth(station(step) * 4 + lax.rem(d, 4)), device_id_type=MESH)

    def offset(v, j):
        first = code_ref[v, 2] * (2 * strip * j + 1 - extent) + extent
        shift = lax.div(first + 128 * extent, 2 * extent) - 64
        return jnp.clip(lax.div(shift + 62, 8) * 8 - 64, -MARGIN, 0) + MARGIN

    def strip_of(step, h, q):
        j = station(step) * 4 + q
        at = jnp.where(first_view, offset(0, j), offset(1, j))
        wide = picture_ref[step, h, pl.ds(pl.multiple_of(q * strip, 16), piece + MARGIN), :]
        part = jnp.where(at == 0, wide[0:piece], wide[8 : 8 + piece])
        return jnp.where(at == MARGIN, wide[MARGIN : MARGIN + piece], part)

    near_tiles = chunk // LANES + 1
    lane_t = lax.broadcasted_iota(jnp.int32, (LANES, LANES), 1)

    def far_shear(step):
        start = pl.multiple_of(station(step) * chunk, LANES)
        for s in range(slabs):
            data = [far_ref[s, :, pl.ds(start + t * LANES, 2 * LANES)] for t in range(near_tiles)]
            spare = (-near_tiles * side) % LANES
            if spare:
                data.append(jnp.zeros((spare, 2 * LANES), jnp.bfloat16))
            moved = lax.dot_general(
                wx_ref[s], jnp.concatenate(data, axis=0), (((1,), (1,)), ((), ())), preferred_element_type=jnp.float32)
            for v in range(VIEWS):
                for t in range(near_tiles):
                    at = t * side // LANES * LANES
                    part = moved[v * LANES : (v + 1) * LANES, at : at + LANES]
                    if side < LANES:
                        part = jnp.where(lane_t // side == t * side % LANES // side, part, 0.0)
                    moved_ref[v, s, pl.ds(start + t * LANES, LANES), LANES : 2 * LANES] = part.astype(jnp.bfloat16)

    def render(step, h):
        start = pl.multiple_of(station(step) * chunk + LANES // 2 - MARGIN, 16)
        kinds = 2 if needs_far[h] else 1
        for k in range(slabs):
            data = [
                moved_ref[v, slab_at(v, k), pl.ds(start, reach), kind * LANES : (kind + 1) * LANES]
                for kind in range(kinds) for v in range(VIEWS)]
            sheared_ref[h, k] = jnp.dot(
                jnp.concatenate(data, axis=1), wy_ref[h, k, 0 : kinds * VIEWS * LANES, :],
                preferred_element_type=jnp.float32)
        for q in range(0, reach, 32):
            part = slice(q, q + 32)
            picture = sheared_ref[h, 0, part, 0:LANES]
            for k in range(1, slabs):
                picture = sheared_ref[h, k, part, 0:LANES] + (
                    1.0 - sheared_ref[h, k, part, LANES : 2 * LANES]) * picture
            picture_ref[step, h, part] = picture
        for i in range(2):
            s1_ref[step, h, i] = strip_of(step, h, 2 * i + 1 - core).astype(jnp.bfloat16)
        first_copy(step, h).start()

    def merge1(step, h):
        ahead = facing_s == 1 - core
        for q, keep in ((1 - col, False), (col, True)):
            near = strip_of(step, h, 2 * q + core)
            both = over(ahead, near, r1_ref[step, h, q].astype(jnp.float32))
            if keep:
                k2_ref[step, h] = both
            else:
                s2_ref[step, h] = both.astype(jnp.bfloat16)

    def merge2(step, h):
        ahead = facing_s == 1 - col
        both = over(ahead, k2_ref[step, h], r2_ref[step, h].astype(jnp.float32))
        if step == stations - 1:
            mine_ref[h] = both
        else:
            s3_ref[step, h] = both.astype(jnp.bfloat16)

    def merges(parts):
        for name, step, h in parts:
            (first_copy if name == "merge1" else second_copy)(step, h).wait()
        for name, step, h in parts:
            (merge1 if name == "merge1" else merge2)(step, h)
        for name, step, h in parts:
            if name == "merge1":
                second_copy(step, h).start()
            elif step < stations - 1:
                third_copy(step, h).start()

    def warp_weights(v):
        column = lax.broadcasted_iota(jnp.int32, (strip, piece), 0)
        source = lax.broadcasted_iota(jnp.int32, (strip, piece), 1) + (offset(v, d) - MARGIN)
        double = float(2 * extent)
        column_in = d * strip + source
        inside = jnp.logical_and(column_in >= 0, column_in < extent)
        num = (code_ref[v, 2] * (2 * (d * strip + column) + 1 - extent) + extent).astype(jnp.float32)
        whole_w = jnp.floor(num / double)
        frac_w = (num - whole_w * double) / double
        tap = lanczos(frac_w - ((source - column).astype(jnp.float32) - whole_w))
        return jnp.where(inside, tap, 0.0)

    def far(step):
        if step in (0, 1, half):
            far_rows((0, 1, half).index(step))
        far_shear(step)

    def finish(h):
        for k in range(1, stations):
            other = lax.rem(z + k, stations)
            pltpu.make_async_remote_copy(
                s3_ref.at[0, h], r3_ref.at[other, h], send3.at[0, h], recv3.at[other, h],
                device_id=at_depth(other * 4 + lax.rem(d, 4)), device_id_type=MESH).wait_recv()
        layers = [
            jnp.where(z == k, mine_ref[h], r3_ref[k, h].astype(jnp.float32)) for k in range(stations)]
        picture = None
        for k in range(stations):
            part = jnp.where(facing_s == 1, layers[stations - 1 - k], layers[k])
            if picture is None:
                picture = part
            else:
                picture = part + (1.0 - replicate_alpha(part, lane_s)) * picture
        composite_ref[lax.div(row_base[h], MARGIN)] = picture

    def warp():
        weights_ref[0], weights_ref[1] = split(jnp.concatenate([warp_weights(v) for v in range(VIEWS)], axis=0))

    actions = {
        "far": lambda step, h: far(step),
        "render": render,
        "warp": lambda step, h: warp(),
        "finish": lambda step, h: finish(h),
    }
    for group in schedule(stations, needs_far[0]):
        if group[0][0] in actions:
            for name, step, h in group:
                actions[name](step, h)
        else:
            merges(group)
    for step in range(stations - 1):
        for h in range(2):
            third_copy(step, h).wait_send()


def warp_kernel(weights_ref, composite_ref, out_ref):
    strip, rows = out_ref.shape[2], out_ref.shape[1] // 4
    crossed = (((0,), (1,)), ((), ()))
    wh, wl = weights_ref[0], weights_ref[1]
    for g in range(2):
        ph, plow = split(composite_ref[g])
        final = (
            lax.dot_general(ph, wh, crossed, preferred_element_type=jnp.float32)
            + lax.dot_general(plow, wh, crossed, preferred_element_type=jnp.float32)
            + lax.dot_general(ph, wl, crossed, preferred_element_type=jnp.float32))
        for v in range(VIEWS):
            for c in range(4):
                row = (v * 4 + c) * MARGIN
                out_ref[v, c * rows + g * MARGIN : c * rows + (g + 1) * MARGIN, :] = (
                    final[row : row + MARGIN, v * strip : (v + 1) * strip])


def body(volume, tf_table, view_code):
    depth_size, band_size = lax.axis_size("depth"), lax.axis_size("band")
    slabs, rows, extent = volume.shape
    stations = depth_size // 4
    chunk = extent // stations
    strip = chunk // 4
    reach = chunk + 2 * MARGIN
    piece = strip + MARGIN
    slots = 1 if band_size == 2 else 2
    padded = extent + 2 * PAD
    bf16, f32 = jnp.bfloat16, jnp.float32
    vmem, anywhere = pl.BlockSpec(memory_space=pltpu.VMEM), pl.BlockSpec(memory_space=pltpu.HBM)
    dma = pltpu.SemaphoreType.DMA
    composite, weights = pl.pallas_call(
        functools.partial(kernel, (depth_size, band_size)),
        out_shape=[
            pltpu.VMEM((2, piece, LANES), f32), pltpu.VMEM((2, VIEWS * strip, piece), bf16)],
        in_specs=[anywhere] * 3,
        out_specs=[vmem, vmem],
        scratch_shapes=[
            pltpu.SMEM(view_code.shape, jnp.int32),
            pltpu.VMEM(volume.shape, jnp.int32),
            pltpu.VMEM(tf_table.shape, jnp.int32),
            pltpu.VMEM((2, slabs, MARGIN, extent), bf16),
            pltpu.VMEM((slots, slabs, MARGIN, extent), bf16),
            pltpu.VMEM((slabs, 4 * rows, padded), bf16),
            pltpu.VMEM((slabs, 4 * MARGIN * slots, padded), bf16),
            pltpu.VMEM((slabs, VIEWS * LANES, 2 * LANES), bf16),
            pltpu.VMEM((2, slabs, 2 * VIEWS * LANES, 2 * LANES), bf16),
            pltpu.VMEM((VIEWS, slabs, extent + LANES, 2 * LANES), bf16),
            pltpu.VMEM((2, slabs, reach, 2 * LANES), f32),
            pltpu.VMEM((stations, VIEWS, reach, LANES), f32),
            pltpu.VMEM((stations, VIEWS, 2, piece, LANES), bf16),
            pltpu.VMEM((stations, VIEWS, 2, piece, LANES), bf16),
            pltpu.VMEM((stations, VIEWS, piece, LANES), bf16),
            pltpu.VMEM((stations, VIEWS, piece, LANES), bf16),
            pltpu.VMEM((stations, VIEWS, piece, LANES), f32),
            pltpu.VMEM((stations, VIEWS, piece, LANES), bf16),
            pltpu.VMEM((stations, VIEWS, piece, LANES), bf16),
            pltpu.VMEM((VIEWS, piece, LANES), f32),
            dma((3,)), dma((2, 3)), dma((slots, 3)),
        ] + [dma((stations, VIEWS))] * 6,
        compiler_params=pltpu.CompilerParams(
            collective_id=0, has_side_effects=True, vmem_limit_bytes=48 * 2**20),
    )(view_code, volume, tf_table)
    out = pl.pallas_call(
        warp_kernel,
        out_shape=jax.ShapeDtypeStruct((VIEWS, LANES, strip), f32),
        in_specs=[vmem, vmem],
        out_specs=vmem,
        compiler_params=pltpu.CompilerParams(vmem_limit_bytes=4 * 2**20),
    )(weights, composite)
    return out.reshape(VIEWS, 4, rows, strip).transpose(0, 3, 1, 2)


def solution(mesh):
    P = jax.sharding.PartitionSpec
    placed = (P("depth", "band", None), P(), P())
    return jax.shard_map(
        body, mesh=mesh, in_specs=placed, out_specs=P(None, "depth", None, "band"), check_vma=False
    )
```
